32 devices in a mesh: img: 2 (over x), row: 4 (over y, core), col: 4 (over z).
Axes of the slice: x: 2, y: 2, z: 4, core: 2. Of those that a mesh axis runs over, the one named last changes fastest.
Arguments:
- latent: bfloat16 [8, 4, 64, 64], P('img', None, 'row', 'col'), may hold values from -6 to 6
- cotangent: bfloat16 [8, 8, 64, 64], P('img', None, 'row', 'col'), may hold values from -6 to 6
- cond: float32 [8, 4, 1152], P('img'), may hold values from -6 to 6
- canvas_kind: int32 [8], P('img'), may hold values from 0 to 1
- w_patch: bfloat16 [16, 1152], P('img'), may hold values from -1.5 to 1.5
- w_qkv: bfloat16 [1152, 3456], P('img'), may hold values from -0.1875 to 0.1875
- w_proj: bfloat16 [1152, 1152], P('img'), may hold values from -1.5 to 1.5
- w_up: bfloat16 [1152, 4608], P('img'), may hold values from -0.1875 to 0.1875
- w_down: bfloat16 [4608, 1152], P('img'), may hold values from -0.09375 to 0.09375
- w_ada: bfloat16 [1152, 6912], P('img'), may hold values from -0.1875 to 0.1875
- w_final_ada: bfloat16 [1152, 2304], P('img'), may hold values from -0.1875 to 0.1875
- w_out: bfloat16 [1152, 32], P('img'), may hold values from -0.1875 to 0.1875
Outputs:
- latent_out: float32 [8, 8, 64, 64], P('img', None, 'row', 'col')
- latent_grad: float32 [8, 4, 64, 64], P('img', None, 'row', 'col')
- cond_grad: float32 [8, 4, 1152], P('img')
- g_patch: float32 [16, 1152], P('img')
- g_qkv: float32 [1152, 3456], P('img')
- g_proj: float32 [1152, 1152], P('img')
- g_up: float32 [1152, 4608], P('img')
- g_down: float32 [4608, 1152], P('img')
- g_ada: float32 [1152, 6912], P('img')
- g_final_ada: float32 [1152, 2304], P('img')
- g_out: float32 [1152, 32], P('img')
The draws below stay inside these ranges and needn't reach their ends.
Inputs may be any that keep to these rules, and one draw needn't show every extreme that they name: Canvas n holds one image of 64 x 64 latent pixels when canvas_kind[n] is 0, and four images of 32 x 32 latent pixels in its quadrants when it is 1; tokens attend only within their image, and only cond[n, 0] is used by a canvas of one image.
All inputs are finite; a program needn't handle non-finite values.
Results may differ from the reference program's by a relative error of at most 0.019.
Values may be sent and summed in bfloat16 or wider, within the bound.
No kernel may reach another device: no remote copies, remote signals or barrier semaphores. Data moves between devices by JAX's collectives and lax.ppermute only.
A program may use at most 248 MiB of HBM per device.

```python
import math
import jax
import jax.numpy as jnp
from jax import lax

D = 1152
HEADS = 16
HD = 72
FF = 4608
CH = 4
OC = 8
LAT = 64
CANVASES = 8


def set_ends(array, key, least, top_value):
    longest = array.shape.index(max(array.shape))
    spots = []
    for shift in (0, 1):
        where = [jax.random.randint(jax.random.fold_in(key, axis), (), 0, length) for axis, length in enumerate(array.shape)]
        where[longest] = (where[longest] + shift) % array.shape[longest]
        spots.append(tuple(where))
    return array.at[spots[0]].set(least).at[spots[1]].set(top_value)


def levels(key, extent, cuts, smallest, high):
    level = 1.0
    for axis_at, shards_of in cuts:
        heights = jax.random.uniform(jax.random.fold_in(jax.random.fold_in(key, 6), axis_at), (shards_of,), jnp.float32, smallest / len(cuts), high / len(cuts))
        level = level * jnp.repeat(jnp.exp(heights), extent[axis_at] // shards_of).reshape((-1,) + (1,) * (len(extent) - 1 - axis_at))
    return level


def scatter_about(stream_key, dims, scale, limit, pieces=(), kind=jnp.bfloat16):
    array = jax.random.normal(stream_key, dims, jnp.float32) * scale
    if len(pieces) > 0:
        array = levels(stream_key, dims, pieces, -0.22, 0.18) * array
    return jnp.clip(array, min=-limit, max=limit).astype(kind)


def setup_inputs(seed: int = 0) -> dict:
    seeds = jax.random.split(jax.random.key(seed), 13)
    latent = scatter_about(seeds[0], (CANVASES, CH, LAT, LAT), 1.0, 6.0, ((0, 2), (2, 4), (3, 4)))
    cotangent = scatter_about(seeds[1], (CANVASES, OC, LAT, LAT), 1.0, 6.0, ((0, 2), (2, 4), (3, 4)))
    cond = scatter_about(seeds[2], (CANVASES, 4, D), 1.0, 6.0, ((0, 2),), jnp.float32)
    canvas_kind = set_ends(jax.random.randint(seeds[3], (CANVASES,), 0, 2), jax.random.fold_in(seeds[3], 1), 0, 1).astype(jnp.int32)
    w_patch = scatter_about(seeds[4], (4 * CH, D), (4 * CH) ** -0.5, 1.5, ((0, 2),))
    w_qkv = scatter_about(seeds[5], (D, 3 * D), D ** -0.5, 0.1875, ((0, 2),))
    w_proj = scatter_about(seeds[6], (D, D), (D // 64) ** -0.5, 1.5, ((0, 2),))
    w_up = scatter_about(seeds[7], (D, FF), D ** -0.5, 0.1875, ((0, 2),))
    w_down = scatter_about(seeds[8], (FF, D), FF ** -0.5, 0.09375, ((0, 2),))
    w_ada = scatter_about(seeds[9], (D, 6 * D), D ** -0.5, 0.1875, ((0, 2),))
    w_final_ada = scatter_about(seeds[10], (D, 2 * D), D ** -0.5, 0.1875, ((0, 2),))
    w_out = scatter_about(seeds[11], (D, 4 * OC), D ** -0.5, 0.1875, ((0, 2),))
    return dict(latent=latent, cotangent=cotangent, cond=cond, canvas_kind=canvas_kind, w_patch=w_patch, w_qkv=w_qkv, w_proj=w_proj, w_up=w_up, w_down=w_down, w_ada=w_ada, w_final_ada=w_final_ada, w_out=w_out)


@jax.custom_vjp
def low(v):
    return lax.optimization_barrier(v.astype(jnp.bfloat16)).astype(jnp.float32)

@jax.custom_vjp
def low_back(v):
    return v

def low_keep(v):
    return (low(v), None)

def low_pass(kept, grad):
    return (grad,)

def back_keep(v):
    return (v, None)

def back_low(kept, grad):
    return (low(grad),)
low.defvjp(low_keep, low_pass)
low_back.defvjp(back_keep, back_low)

def matmul(left, right):
    return jnp.dot(left, right, precision=lax.Precision.HIGHEST)

def layer_norm(value):
    center = value - lax.optimization_barrier(jnp.mean(value, -1, keepdims=True))
    spread = lax.optimization_barrier(jnp.mean(center * center, -1, keepdims=True))
    return center * lax.rsqrt(spread + 1e-06)

def swish(value):
    return value * jax.nn.sigmoid(value)

def sincos(coord, count):
    freqs = 1.0 / 10000.0 ** (jnp.arange(count, dtype=jnp.float32) / count)
    angle = coord.astype(jnp.float32)[..., None] * freqs
    return jnp.concatenate([jnp.sin(angle), jnp.cos(angle)], axis=-1)

def canvas_block(lat, kind, cond, weights):
    w_patch, w_qkv, w_proj, w_up, w_down, w_ada, w_final_ada, w_out = weights
    count = lat.shape[0]
    grid = LAT // 2
    half = grid // 2
    tokens = grid * grid
    hi = lax.Precision.HIGHEST
    rolled = jnp.roll(lat, (1, 1), axis=(2, 3))
    patches = rolled.reshape(count, CH, grid, 2, grid, 2).transpose(0, 2, 4, 1, 3, 5).reshape(count * tokens, CH * 4)
    embedded = low_back(matmul(patches, w_patch)).reshape(count, tokens, D)
    prow = jnp.arange(grid, dtype=jnp.int32)[:, None] * jnp.ones((1, grid), jnp.int32)
    pcol = jnp.transpose(prow)
    kind_grid = kind[:, None, None]
    lrow = prow[None] - kind_grid * (prow[None] // half) * half
    lcol = pcol[None] - kind_grid * (pcol[None] // half) * half
    pos = jnp.concatenate([sincos(lcol, D // 4), sincos(lrow, D // 4)], axis=-1).reshape(count, tokens, D)
    quad = (prow // half * 2 + pcol // half).reshape(tokens)
    slot = kind[:, None] * quad[None, :]
    picker = (slot[..., None] == jnp.arange(4, dtype=jnp.int32)).astype(jnp.float32)
    silu_c = low(swish(cond))
    mods = jnp.einsum('nsd,de->nse', silu_c, w_ada, precision=hi)
    fmods = jnp.einsum('nsd,de->nse', silu_c, w_final_ada, precision=hi)
    mod_tok = jnp.einsum('nts,nse->nte', picker, mods, precision=hi)
    fmod_tok = jnp.einsum('nts,nse->nte', picker, fmods, precision=hi)
    shift1, scale1, gate1, shift2, scale2, gate2 = jnp.split(mod_tok, 6, axis=-1)
    shiftf, scalef = jnp.split(fmod_tok, 2, axis=-1)
    x0 = embedded + pos
    a1 = low(layer_norm(x0) * (1.0 + scale1) + shift1)
    qkv = low_back(low(matmul(a1.reshape(-1, D), w_qkv))).reshape(count, tokens, 3 * D)
    query = qkv[..., :D].reshape(count, tokens, HEADS, HD)
    key = qkv[..., D:2 * D].reshape(count, tokens, HEADS, HD)
    value = qkv[..., 2 * D:].reshape(count, tokens, HEADS, HD)
    scores = low_back(jnp.einsum('nqhd,nkhd->nhqk', query, key, precision=hi) * HD ** (-0.5))
    allowed = slot[:, :, None] == slot[:, None, :]
    scores = jnp.where(allowed[:, None], scores, -1e+30)
    top = lax.optimization_barrier(jnp.max(scores, -1, keepdims=True))
    expd = jnp.exp(scores - top)
    prob = expd / lax.optimization_barrier(jnp.sum(expd, -1, keepdims=True))
    att = low_back(low(jnp.einsum('nhqk,nkhd->nqhd', low(prob), value, precision=hi))).reshape(count * tokens, D)
    proj = low_back(matmul(att, w_proj)).reshape(count, tokens, D)
    x1 = x0 + gate1 * proj
    a2 = low(layer_norm(x1) * (1.0 + scale2) + shift2)
    pre = low_back(matmul(a2.reshape(-1, D), w_up))
    hid = low(jax.nn.gelu(pre, approximate=True))
    down = low_back(matmul(hid, w_down)).reshape(count, tokens, D)
    x2 = x1 + gate2 * down
    af = low(layer_norm(x2) * (1.0 + scalef) + shiftf)
    outp = low_back(matmul(af.reshape(-1, D), w_out))
    tile = outp.reshape(count, grid, grid, OC, 2, 2).transpose(0, 3, 1, 4, 2, 5).reshape(count, OC, LAT, LAT)
    return jnp.roll(tile, (-1, -1), axis=(2, 3))

def reference(latent, cotangent, cond, canvas_kind, w_patch, w_qkv, w_proj, w_up, w_down, w_ada, w_final_ada, w_out):
    weights = (w_patch.astype(jnp.float32), w_qkv.astype(jnp.float32), w_proj.astype(jnp.float32), w_up.astype(jnp.float32), w_down.astype(jnp.float32), w_ada.astype(jnp.float32), w_final_ada.astype(jnp.float32), w_out.astype(jnp.float32))
    group = math.gcd(CANVASES, 4)
    rounds = CANVASES // group
    kinds = canvas_kind.reshape(rounds, group)

    def forward(lat, cnd, wts):

        def one(carry, items):
            piece, kind, cpiece = items
            return (carry, canvas_block(piece, kind, cpiece, wts))
        _, outs = lax.scan(jax.checkpoint(one), jnp.zeros((), jnp.float32), (lat.reshape(rounds, group, CH, LAT, LAT), kinds, cnd.reshape(rounds, group, 4, D)))
        return outs.reshape(CANVASES, OC, LAT, LAT)
    latent_out, pull = jax.vjp(forward, latent.astype(jnp.float32), cond, weights)
    latent_grad, cond_grad, grads = pull(cotangent.astype(jnp.float32))
    return (latent_out, latent_grad, cond_grad, grads[0], grads[1], grads[2], grads[3], grads[4], grads[5], grads[6], grads[7])
```

```python
import math

import jax
import jax.numpy as jnp
from jax import lax
from jax.experimental import pallas as pl
from jax.experimental.pallas import tpu as pltpu
from jax.sharding import PartitionSpec as P

HEADS = 16
RC = ("row", "col")
BF = jnp.bfloat16
F32 = jnp.float32


def shifted(block, axis, distance):
    size = lax.axis_size(axis)
    return lax.ppermute(block, axis, [((i - distance) % size, i) for i in range(size)])


def layer_norm(value):
    center = value - jnp.mean(value, -1, keepdims=True)
    spread = jnp.mean(center * center, -1, keepdims=True)
    return center * lax.rsqrt(spread + 1e-06)


def modulate(value, shift, scale):
    return layer_norm(value) * (1.0 + scale[:, None, :]) + shift[:, None, :]


def gelu_tanh(value):
    return jax.nn.gelu(value, approximate=True)


def swish(value):
    return value * jax.nn.sigmoid(value)


def sincos(coord, count):
    freqs = 1.0 / 10000.0 ** (jnp.arange(count, dtype=F32) / count)
    angle = coord.astype(F32)[..., None] * freqs
    return jnp.concatenate([jnp.sin(angle), jnp.cos(angle)], axis=-1)


def dotd(left, right, ldim, rdim):
    return lax.dot_general(
        left, right, (((ldim,), (rdim,)), ((), ())), preferred_element_type=F32
    )


def send_down(value, k):
    size = lax.axis_size("img")
    return lax.ppermute(value, "img", [(j, (j - k) % size) for j in range(size)])


def send_up(value, k):
    size = lax.axis_size("img")
    return lax.ppermute(value, "img", [(j, (j + k) % size) for j in range(size)])


def split_own(value, axis):
    size = lax.axis_size("img")
    me = lax.axis_index("img")
    width = value.shape[axis] // size
    blocks = [lax.slice_in_dim(value, i * width, (i + 1) * width, axis=axis) for i in range(size)]
    if size == 2:
        return [
            jnp.where(me == 0, blocks[0], blocks[1]),
            jnp.where(me == 0, blocks[1], blocks[0]),
        ]
    return [
        lax.dynamic_slice_in_dim(value, (me + k) % size * width, width, axis=axis)
        for k in range(size)
    ]


def join_own(items, axis):
    size = lax.axis_size("img")
    me = lax.axis_index("img")
    if size == 2:
        return jnp.concatenate(
            [jnp.where(me == 0, items[0], items[1]), jnp.where(me == 0, items[1], items[0])],
            axis=axis,
        )
    width = items[0].shape[axis]
    twice = jnp.concatenate(list(items) + list(items), axis=axis)
    return lax.dynamic_slice_in_dim(twice, (size - me) % size * width, size * width, axis=axis)


def tied(value, *after):
    return lax.optimization_barrier((value, after))[0]


def swap_parts(parts):
    size = len(parts)
    return [parts[0]] + [send_down(parts[size - k], k) for k in range(1, size)]


def swap_full(value):
    return [value] + [send_down(value, k) for k in range(1, lax.axis_size("img"))]


def other_rows(weight):
    size = lax.axis_size("img")
    tiles = lax.axis_size("row") * lax.axis_size("col")
    at = lax.axis_index("row") * lax.axis_size("col") + lax.axis_index("col")
    rows, width = weight.shape
    each = -(-rows // (tiles * 8)) * 8
    start = jnp.minimum(at * each, rows - each)
    piece = lax.dynamic_slice(weight, (start, 0), (each, width))
    if rows % each:
        lag = jnp.clip(at * each - start, 0, each)
        piece = lax.dynamic_slice(jnp.concatenate([piece, piece], 0), (lag, 0), (each, width))
    pieces = [send_down(piece, k) for k in range(1, size)]
    if size == 2:
        return [lax.all_gather(pieces[0], RC, axis=0, tiled=True)], pieces
    full = lax.all_gather(jnp.stack(pieces), RC, axis=1, tiled=True)
    return [full[k] for k in range(size - 1)], pieces


def widened(part, rows, axis):
    extra = rows - part.shape[axis]
    if extra == 0:
        return part
    pads = [(0, 0), (0, 0)]
    pads[axis] = (0, extra)
    return jnp.pad(part, pads)


def quad_order(rows_n, cols_n):
    def quad(s):
        return s // cols_n * 2 // rows_n * 2 + s % cols_n * 2 // cols_n

    return sorted(range(rows_n * cols_n), key=quad)


def pick_tokens(pieces, par, half):
    lane = lax.broadcasted_iota(jnp.int32, pieces[0].shape, 1)
    tiles = []
    for j in range(0, len(pieces), 2):
        a = pieces[j].astype(F32)
        b = pieces[j + 1].astype(F32)
        if par == 0:
            tile = jnp.where(lane < half, a, pltpu.roll(b, half, 1))
        else:
            tile = jnp.where(lane < half, pltpu.roll(a, half, 1), b)
        tiles.append(tile.astype(BF))
    return jnp.concatenate(tiles, axis=1)


def put_tokens(first, second, spot, half):
    tile = spot // 2
    a = first[:, tile * 2 * half : (tile + 1) * 2 * half]
    b = second[:, tile * 2 * half : (tile + 1) * 2 * half]
    lane = lax.broadcasted_iota(jnp.int32, a.shape, 1)
    if spot % 2 == 0:
        return jnp.where(lane < half, a, pltpu.roll(b, half, 1))
    return jnp.where(lane < half, pltpu.roll(a, half, 1), b)


def attend_kernel(order, half, factor, kind_ref, x_ref, o_ref, lse_ref, qkv_s, o_s):
    step = pl.program_id(1)
    count = len(order) * half
    block = count // 4
    coef = factor * math.log2(math.e)
    for par in range(2):
        for c in range(3):
            qkv_s[c] = pick_tokens([x_ref[s, 0, c] for s in order], par, half)
        single = kind_ref[2 * step + par] == 0
        for b in range(4):
            cols = slice(b * block, (b + 1) * block)

            def work(keys, cols=cols, par=par):
                query = qkv_s[0, :, cols]
                score = dotd(qkv_s[1, :, keys], query, 0, 0)
                top = jnp.max(score, axis=0, keepdims=True)
                expd = jnp.exp2((score - top) * coef)
                total = jnp.sum(expd, axis=0, keepdims=True)
                out = dotd(qkv_s[2, :, keys], expd.astype(BF), 1, 0)
                o_s[par, :, cols] = out * (1.0 / total)
                lse_ref[0, par, :, cols] = top * coef + jnp.log2(total)

            @pl.when(single)
            def _():
                work(slice(0, count))

            @pl.when(jnp.logical_not(single))
            def _():
                work(cols)

    for i, s in enumerate(order):
        o_ref[s, 0] = put_tokens(o_s[0], o_s[1], i, half).astype(BF)


def attend_back_kernel(
    order, half, factor, kind_ref, x_ref, d_ref, lse_ref, g_ref, qkv_s, d_s, g_s
):
    step = pl.program_id(1)
    count = len(order) * half
    block = count // 4
    coef = factor * math.log2(math.e)
    for par in range(2):
        for c in range(3):
            qkv_s[c] = pick_tokens([x_ref[s, 0, c] for s in order], par, half)
        d_s[...] = pick_tokens([d_ref[s, 0] for s in order], par, half)
        single = kind_ref[2 * step + par] == 0
        for b in range(4):
            cols = slice(b * block, (b + 1) * block)

            def work(keys, fresh, cols=cols, par=par):
                query = qkv_s[0, :, cols]
                dout = d_s[:, cols]
                score = dotd(qkv_s[1, :, keys], query, 0, 0)
                prob = jnp.exp2(score * coef - lse_ref[0, par, :, cols])
                dprob = dotd(qkv_s[2, :, keys], dout, 0, 0)
                delta = jnp.sum(prob * dprob, axis=0, keepdims=True)
                dscore = (prob * (dprob - delta)).astype(BF)
                g_s[par, 0, :, cols] = dotd(qkv_s[1, :, keys], dscore, 1, 0) * factor
                dkey = dotd(query, dscore, 1, 1) * factor
                dvalue = dotd(dout, prob.astype(BF), 1, 1)
                if fresh:
                    g_s[par, 1, :, keys] = dkey
                    g_s[par, 2, :, keys] = dvalue
                else:
                    g_s[par, 1, :, keys] += dkey
                    g_s[par, 2, :, keys] += dvalue

            @pl.when(single)
            def _():
                work(slice(0, count), b == 0)

            @pl.when(jnp.logical_not(single))
            def _():
                work(cols, True)

    for c in range(3):
        for i, s in enumerate(order):
            g_ref[s, 0, c] = put_tokens(g_s[0, c], g_s[1, c], i, half).astype(BF)


def attend(kinds, x, order, half, factor):
    tiles, per, _, depth, tokens = x.shape
    count = tiles * half
    pairs = tokens // (2 * half)
    return pl.pallas_call(
        lambda *refs: attend_kernel(order, half, factor, *refs),
        grid_spec=pltpu.PrefetchScalarGridSpec(
            num_scalar_prefetch=1,
            grid=(per, pairs),
            in_specs=[
                pl.BlockSpec((tiles, 1, 3, depth, 2 * half), lambda h, p, kd: (0, h, 0, 0, p))
            ],
            out_specs=[
                pl.BlockSpec((tiles, 1, depth, 2 * half), lambda h, p, kd: (0, h, 0, p)),
                pl.BlockSpec((1, 2, 1, count), lambda h, p, kd: (h, p, 0, 0)),
            ],
            scratch_shapes=[
                pltpu.VMEM((3, depth, count), BF),
                pltpu.VMEM((2, depth, count), F32),
            ],
        ),
        out_shape=[
            jax.ShapeDtypeStruct((tiles, per, depth, tokens), BF),
            jax.ShapeDtypeStruct((per, 2 * pairs, 1, count), F32),
        ],
        name="attend",
        cost_estimate=pl.CostEstimate(
            flops=10**10, bytes_accessed=4 * 10**7, transcendentals=per * tokens * count
        ),
    )(kinds, x)


def attend_back(kinds, x, d, lse, order, half, factor):
    tiles, per, _, depth, tokens = x.shape
    count = tiles * half
    pairs = tokens // (2 * half)
    return pl.pallas_call(
        lambda *refs: attend_back_kernel(order, half, factor, *refs),
        grid_spec=pltpu.PrefetchScalarGridSpec(
            num_scalar_prefetch=1,
            grid=(per, pairs),
            in_specs=[
                pl.BlockSpec((tiles, 1, 3, depth, 2 * half), lambda h, p, kd: (0, h, 0, 0, p)),
                pl.BlockSpec((tiles, 1, depth, 2 * half), lambda h, p, kd: (0, h, 0, p)),
                pl.BlockSpec((1, 2, 1, count), lambda h, p, kd: (h, p, 0, 0)),
            ],
            out_specs=pl.BlockSpec(
                (tiles, 1, 3, depth, 2 * half), lambda h, p, kd: (0, h, 0, 0, p)
            ),
            scratch_shapes=[
                pltpu.VMEM((3, depth, count), BF),
                pltpu.VMEM((depth, count), BF),
                pltpu.VMEM((2, 3, depth, count), F32),
            ],
        ),
        out_shape=jax.ShapeDtypeStruct(x.shape, BF),
        name="attend_back",
        cost_estimate=pl.CostEstimate(
            flops=10**10, bytes_accessed=4 * 10**7, transcendentals=per * tokens * count
        ),
    )(kinds, x, d, lse)


def swapped(value, axis, bit):
    return lax.ppermute(value, axis, [(j, j ^ bit) for j in range(lax.axis_size(axis))])


def added(a, b):
    return (a.astype(F32) + b.astype(F32)).astype(BF)


def halved(value, axis, bit):
    upper = lax.axis_index(axis) // bit % 2
    rows = value.shape[0] // 2
    keep = lax.dynamic_slice_in_dim(value, upper * rows, rows, 0)
    give = lax.dynamic_slice_in_dim(value, (1 - upper) * rows, rows, 0)
    return added(keep, swapped(give, axis, bit))


def doubled(value, axis, bit):
    upper = lax.axis_index(axis) // bit % 2
    got = swapped(value, axis, bit)
    return jnp.where(
        upper == 0, jnp.concatenate([value, got], 0), jnp.concatenate([got, value], 0)
    )


def bits_of(axis):
    return [(axis, 1 << i) for i in range(lax.axis_size(axis).bit_length() - 1)]


def tile_sum(value, cols_first):
    rows, cols = bits_of("row"), bits_of("col")
    if cols_first:
        halves, wholes = rows[:1] + cols[:-1], cols[-1:] + rows[1:]
    else:
        halves, wholes = rows + cols[:-1], cols[-1:]
    for axis, bit in halves:
        value = halved(value, axis, bit)
    for axis, bit in wholes:
        value = added(value, swapped(value, axis, bit))
    for axis, bit in halves[::-1]:
        value = doubled(value, axis, bit)
    return value


def exchange(x):
    return lax.all_to_all(x, RC, split_axis=0, concat_axis=0, tiled=True)


def summed_apart(small, items, finish):
    once = 1 + jnp.minimum(lax.axis_index("row"), 0)
    tiles, each, width = small.shape
    imgs = lax.axis_size("img")

    def body(_, state):
        parts = jnp.sum(exchange(state[0][0]).astype(F32), axis=0).astype(BF)
        parts = jnp.stack(swap_full(parts))
        parts = exchange(jnp.broadcast_to(parts[None], (tiles,) + parts.shape))
        parts = parts.transpose(1, 0, 2, 3)
        done = finish(parts.reshape(imgs, tiles * each, width))
        return parts, done, [tile_sum(value, c % 2 == 1) for c, value in enumerate(state[2])]

    start = jnp.broadcast_to(small[None], (imgs,) + small.shape)
    empty = jax.eval_shape(finish, jax.ShapeDtypeStruct((imgs, tiles * each, width), BF))
    empty = jnp.zeros(empty.shape, empty.dtype)
    small, done, items = lax.fori_loop(0, once, body, (start, empty, items))
    return small.reshape(imgs, tiles * each, width), done, items


def outer_kernel(left_ref, right_ref, out_ref):
    out_ref[...] = dotd(left_ref[...], right_ref[...], 0, 0)


def outer(left, right, block):
    depth, rows = left.shape
    cols = right.shape[1]
    return pl.pallas_call(
        outer_kernel,
        grid=(cols // block,),
        in_specs=[
            pl.BlockSpec((depth, rows), lambda j: (0, 0)),
            pl.BlockSpec((depth, block), lambda j: (0, j)),
        ],
        out_specs=pl.BlockSpec((rows, block), lambda j: (0, j)),
        out_shape=jax.ShapeDtypeStruct((rows, cols), F32),
        name="outer",
    )(left, right)


def local(
    latent,
    cotangent,
    cond,
    canvas_kind,
    w_patch,
    w_qkv,
    w_proj,
    w_up,
    w_down,
    w_ada,
    w_final_ada,
    w_out,
):
    local_n, chans, tile_r, tile_c = latent.shape
    out_ch = cotangent.shape[1]
    slots = cond.shape[1]
    width = cond.shape[2]
    inner = w_up.shape[1]
    imgs = lax.axis_size("img")
    rows_n = lax.axis_size("row")
    cols_n = lax.axis_size("col")
    row_at = lax.axis_index("row")
    col_at = lax.axis_index("col")
    tiles = rows_n * cols_n
    patch_r = tile_r // 2
    patch_c = tile_c // 2
    tile_tok = patch_r * patch_c
    half = patch_r * rows_n // 2
    half_c = patch_c * cols_n // 2
    head_dim = width // HEADS
    per = HEADS // tiles
    factor = head_dim ** (-0.5)
    rows = local_n * tile_tok
    order = quad_order(rows_n, cols_n)

    o_qkv, sent = other_rows(w_qkv)
    w_straight = tied(w_proj, sent)
    o_proj = [send_down(w_straight, k) for k in range(1, imgs)]
    o_up, sent = other_rows(tied(w_up, sent))
    o_down, _ = other_rows(tied(w_down, sent))
    wp = join_own([w_patch] + [send_down(w_patch, k) for k in range(1, imgs)], 0)
    wout = join_own([w_out] + [send_down(w_out, k) for k in range(1, imgs)], 0)

    stacked = jnp.concatenate([latent, cotangent], axis=1)
    upper = shifted(stacked[:, :, -1:, :], "row", 1)
    framed = jnp.concatenate([upper, stacked[:, :, :-1, :]], axis=2)
    beside = shifted(framed[:, :, :, -1:], "col", 1)
    framed = jnp.concatenate([beside, framed[:, :, :, :-1]], axis=3)

    def to_tokens(tile):
        depth = tile.shape[1]
        shaped = tile.reshape(local_n, depth, patch_r, 2, patch_c, 2).transpose(0, 2, 4, 1, 3, 5)
        return shaped.reshape(rows, depth * 4)

    def to_tile(tokens):
        depth = tokens.shape[1] // 4
        shaped = tokens.reshape(local_n, patch_r, patch_c, depth, 2, 2).transpose(0, 3, 1, 4, 2, 5)
        return shaped.reshape(local_n, depth, tile_r, tile_c)

    pieces = to_tokens(framed[:, :chans])
    dout = to_tokens(framed[:, chans:])

    quad = row_at * 2 // rows_n * 2 + col_at * 2 // cols_n
    slot = canvas_kind * quad
    picker = (slot[:, None] == jnp.arange(slots, dtype=jnp.int32)[None, :]).astype(F32)
    silu = swish(cond)
    silu_low = silu.astype(BF)
    chosen = jnp.sum(picker[:, :, None] * silu_low.astype(F32), axis=1).astype(BF)
    packed = jnp.concatenate([chosen, silu_low.reshape(local_n * slots, width)], axis=0)
    packed = swap_parts(split_own(packed, 1))
    silu_all = jnp.concatenate([item[local_n:] for item in packed], axis=0)
    chosen_all = jnp.concatenate([item[:local_n] for item in packed], axis=0)
    part = jnp.concatenate(
        [dotd(chosen_all, w_ada, 1, 0), dotd(chosen_all, w_final_ada, 1, 0)], axis=1
    )
    part = [part[k * local_n : (k + 1) * local_n] for k in range(imgs)]
    mods = part[0]
    for k in range(1, imgs):
        mods = mods + send_up(part[k], k)
    shift1, scale1, gate1, shift2, scale2, gate2, shiftf, scalef = jnp.split(mods, 8, axis=-1)

    prow = row_at * patch_r + jnp.arange(patch_r, dtype=jnp.int32)
    pcol = col_at * patch_c + jnp.arange(patch_c, dtype=jnp.int32)
    lrow = prow[None, :] - canvas_kind[:, None] * (prow[None, :] // half) * half
    lcol = pcol[None, :] - canvas_kind[:, None] * (pcol[None, :] // half_c) * half_c
    table_r = sincos(lrow, width // 4)
    table_c = sincos(lcol, width // 4)
    full = (local_n, patch_r, patch_c, width // 2)
    positions = jnp.concatenate(
        [
            jnp.broadcast_to(table_c[:, None, :, :], full),
            jnp.broadcast_to(table_r[:, :, None, :], full),
        ],
        axis=-1,
    ).reshape(local_n, tile_tok, width)

    def tokens3(value):
        return value.reshape(local_n, tile_tok, -1)

    x0 = tokens3(dotd(pieces, wp, 1, 0)) + positions
    a1 = modulate(x0, shift1, scale1).astype(BF).reshape(rows, width)
    a1_parts = split_own(a1, 1)
    a1_all = jnp.concatenate(swap_parts(a1_parts), 0)

    def product(parts, own, others):
        total = dotd(parts[0], own, 1, 0)
        for part, other in zip(parts[1:], others):
            total = total + dotd(widened(part, other.shape[0], 1), other, 1, 0)
        return total

    def back_product(value, own, others):
        items = [dotd(value, own, 1, 1)]
        for other in others:
            items.append(dotd(value, other, 1, 1)[:, : own.shape[0]])
        return items

    qkv = dotd(w_qkv, a1_parts[0], 0, 1)
    for part, other in zip(a1_parts[1:], o_qkv):
        qkv = qkv + dotd(other, widened(part, other.shape[0], 1), 0, 1)
    qkv = qkv.astype(BF).reshape(3, tiles, per, head_dim, rows).transpose(1, 2, 0, 3, 4)
    qkv = exchange(qkv)
    qkv, o_proj = lax.optimization_barrier((qkv, o_proj))
    att, lse = attend(canvas_kind, qkv, order, tile_tok, factor)
    att = exchange(att).reshape(width, rows)
    att, a1_all = lax.optimization_barrier((att, a1_all))
    att_parts = split_own(att, 0)
    att_all = jnp.concatenate(swap_parts(att_parts), 1)
    proj = dotd(att_parts[0], w_proj, 0, 0)
    for part, other in zip(att_parts[1:], o_proj):
        proj = proj + dotd(widened(part, other.shape[0], 0), other, 0, 0)
    proj = tokens3(proj)
    x1 = x0 + gate1[:, None, :] * proj
    a2 = modulate(x1, shift2, scale2).astype(BF).reshape(rows, width)
    a2_parts = split_own(a2, 1)
    a2_all = jnp.concatenate(swap_parts(a2_parts), 0)
    pre = product(a2_parts, w_up, o_up)
    hid = gelu_tanh(pre).astype(BF)
    hid, att_all, a2_all = lax.optimization_barrier((hid, att_all, a2_all))
    hid_parts = split_own(hid, 1)
    hid_all = jnp.concatenate(swap_parts(hid_parts), 0)
    down = tokens3(product(hid_parts, w_down, o_down))
    x2 = x1 + gate2[:, None, :] * down
    af = modulate(x2, shiftf, scalef).astype(BF).reshape(rows, width)
    outp = dotd(af, wout, 1, 0)

    g_out = dotd(dout, af, 0, 0)
    daf = tokens3(dotd(dout, wout, 1, 1))
    _, pull = jax.vjp(modulate, x2, shiftf, scalef)
    dx2, dshiftf, dscalef = pull(daf)
    dgate2 = jnp.sum(dx2 * down, axis=1)
    ddown = (gate2[:, None, :] * dx2).astype(BF).reshape(rows, width)
    ddown_all = jnp.concatenate(swap_full(ddown), 0)
    dhid = join_own(back_product(ddown, w_down, o_down), 1)
    _, pull = jax.vjp(gelu_tanh, pre)
    dpre = pull(dhid)[0].astype(BF)
    dpre, hid_all = lax.optimization_barrier((dpre, hid_all))
    dpre_all = jnp.concatenate(swap_full(dpre), 0)
    da2 = tokens3(join_own(back_product(dpre, w_up, o_up), 1))
    da2, ddown_all = lax.optimization_barrier((da2, ddown_all))
    g_down = dotd(hid_all, ddown_all, 0, 0).astype(BF)
    da2, g_down = lax.optimization_barrier((da2, g_down))
    g_down = lax.psum_scatter(g_down, RC, scatter_dimension=0, tiled=True)
    _, pull = jax.vjp(modulate, x1, shift2, scale2)
    dx1_norm, dshift2, dscale2 = pull(da2)
    dx1 = dx2 + dx1_norm
    dgate1 = jnp.sum(dx1 * proj, axis=1)
    dproj = (gate1[:, None, :] * dx1).astype(BF).reshape(rows, width)
    datt = [dotd(w_proj, dproj, 1, 1)]
    for other in o_proj:
        datt.append(dotd(other, dproj, 1, 1)[: w_proj.shape[0]])
    datt = join_own(datt, 0).astype(BF)
    datt = exchange(datt.reshape(tiles, per, head_dim, rows))
    dproj_all = jnp.concatenate(swap_full(dproj), 0)
    dqkv = attend_back(canvas_kind, qkv, datt, lse, order, tile_tok, factor)
    dqkv, dpre_all = lax.optimization_barrier((dqkv, dpre_all))
    dqkv = exchange(dqkv)
    g_up = dotd(a2_all, dpre_all, 0, 0).astype(BF)
    dqkv, g_up, g_down, dproj_all = lax.optimization_barrier((dqkv, g_up, g_down, dproj_all))
    g_down = lax.all_gather(g_down, RC, axis=0, tiled=True)
    dqkv = dqkv.transpose(2, 0, 1, 3, 4).reshape(3 * width, rows)
    dqkv_all = jnp.concatenate(swap_full(dqkv), 1)
    dqkv_all, g_up, g_down = lax.optimization_barrier((dqkv_all, g_up, g_down))
    g_up = lax.psum(g_up, RC)
    da1 = [dotd(dqkv, w_qkv, 0, 1)]
    for other in o_qkv:
        da1.append(dotd(dqkv, other, 0, 1)[:, : w_qkv.shape[0]])
    da1 = tokens3(join_own(da1, 1))
    g_proj = dotd(att_all, dproj_all, 1, 0).astype(BF)
    g_att = [
        dotd(a1_all, dqkv_all[c * width : (c + 1) * width], 0, 1).astype(BF) for c in range(3)
    ]
    _, pull = jax.vjp(modulate, x0, shift1, scale1)
    dx0_norm, dshift1, dscale1 = pull(da1)
    dtok = (dx1 + dx0_norm).astype(BF).reshape(rows, width)
    g_patch = dotd(pieces, dtok, 0, 0)
    dpatch = dotd(dtok, wp, 1, 1)

    dmods = jnp.concatenate(
        [dshift1, dscale1, dgate1, dshift2, dscale2, dgate2, dshiftf, dscalef], axis=-1
    )
    dmods = (picker[:, :, None] * dmods[:, None, :]).reshape(local_n * slots * 8, width)
    small = jnp.concatenate([g_patch, g_out, dmods], axis=0)
    n_patch = g_patch.shape[0]
    n_out = g_out.shape[0]
    count = small.shape[0]
    each = -(-count // tiles)
    small = jnp.pad(small, ((0, each * tiles - count), (0, 0))).astype(BF)
    step = local_n * slots

    def split_small(value):
        return value[:, n_patch + n_out : count].reshape(imgs * step, 8 * width)

    def back_cond(value):
        dmods = split_small(value)
        dsilu = dotd(dmods[:, : 6 * width], w_ada, 1, 1)
        dsilu = dsilu + dotd(dmods[:, 6 * width :], w_final_ada, 1, 1)
        dsilu = [dsilu[k * step : (k + 1) * step] for k in range(imgs)]
        dsilu = [dsilu[0]] + [send_up(dsilu[imgs - k], imgs - k) for k in range(1, imgs)]
        return join_own(dsilu, 1)

    small, dsilu, g_att = summed_apart(
        small.reshape(tiles, each, width), g_att + [g_proj], back_cond
    )
    g_qkv = jnp.concatenate(g_att[:3], axis=1)
    g_proj = g_att[3]
    sums = jnp.sum(small[:, : n_patch + n_out].astype(F32), axis=0)
    g_patch = split_own(sums[:n_patch], 0)[0]
    g_out = split_own(sums[n_patch:], 1)[0].T
    dmods = split_small(small)
    g_ada = outer(silu_all, dmods[:, : 6 * width], width)
    g_fada = outer(silu_all, dmods[:, 6 * width :], width)
    dsilu = dsilu.reshape(local_n, slots, width)
    _, pull = jax.vjp(swish, cond)
    cond_grad = pull(dsilu)[0]

    joined = jnp.concatenate([to_tile(outp), to_tile(dpatch)], axis=1)
    right_rim = shifted(joined[:, :, :, :1], "col", -1)
    joined = jnp.concatenate([joined[:, :, :, 1:], right_rim], axis=3)
    lower_rim = shifted(joined[:, :, :1, :], "row", -1)
    joined = jnp.concatenate([joined[:, :, 1:, :], lower_rim], axis=2)
    return (
        joined[:, :out_ch],
        joined[:, out_ch:],
        cond_grad,
        g_patch,
        g_qkv.astype(F32),
        g_proj.astype(F32),
        g_up.astype(F32),
        g_down.astype(F32),
        g_ada,
        g_fada,
        g_out,
    )


def solution(mesh):
    rows = P("img", None)
    tile = P("img", None, "row", "col")
    whole = P("img", None, None)
    return jax.shard_map(
        local,
        mesh=mesh,
        in_specs=(tile, tile, whole, P("img")) + (rows,) * 8,
        out_specs=(tile, tile, whole) + (rows,) * 8,
        check_vma=False,
    )
```

```python
import math

import jax
import jax.numpy as jnp
from jax import lax
from jax.experimental import pallas as pl
from jax.experimental.pallas import tpu as pltpu
from jax.sharding import PartitionSpec as P

HEADS = 16
RC = ("row", "col")
BF = jnp.bfloat16
F32 = jnp.float32


def shifted(block, axis, distance):
    size = lax.axis_size(axis)
    return lax.ppermute(block, axis, [((i - distance) % size, i) for i in range(size)])


def layer_norm(value):
    center = value - jnp.mean(value, -1, keepdims=True)
    spread = jnp.mean(center * center, -1, keepdims=True)
    return center * lax.rsqrt(spread + 1e-06)


def modulate(value, shift, scale):
    return layer_norm(value) * (1.0 + scale[:, None, :]) + shift[:, None, :]


def gelu_tanh(value):
    return jax.nn.gelu(value, approximate=True)


def swish(value):
    return value * jax.nn.sigmoid(value)


def sincos(coord, count):
    freqs = 1.0 / 10000.0 ** (jnp.arange(count, dtype=F32) / count)
    angle = coord.astype(F32)[..., None] * freqs
    return jnp.concatenate([jnp.sin(angle), jnp.cos(angle)], axis=-1)


def dotd(left, right, ldim, rdim):
    return lax.dot_general(
        left, right, (((ldim,), (rdim,)), ((), ())), preferred_element_type=F32
    )


def send_down(value, k):
    size = lax.axis_size("img")
    return lax.ppermute(value, "img", [(j, (j - k) % size) for j in range(size)])


def send_up(value, k):
    size = lax.axis_size("img")
    return lax.ppermute(value, "img", [(j, (j + k) % size) for j in range(size)])


def split_own(value, axis):
    size = lax.axis_size("img")
    me = lax.axis_index("img")
    width = value.shape[axis] // size
    blocks = [lax.slice_in_dim(value, i * width, (i + 1) * width, axis=axis) for i in range(size)]
    if size == 2:
        return [
            jnp.where(me == 0, blocks[0], blocks[1]),
            jnp.where(me == 0, blocks[1], blocks[0]),
        ]
    return [
        lax.dynamic_slice_in_dim(value, (me + k) % size * width, width, axis=axis)
        for k in range(size)
    ]


def join_own(items, axis):
    size = lax.axis_size("img")
    me = lax.axis_index("img")
    if size == 2:
        return jnp.concatenate(
            [jnp.where(me == 0, items[0], items[1]), jnp.where(me == 0, items[1], items[0])],
            axis=axis,
        )
    width = items[0].shape[axis]
    twice = jnp.concatenate(list(items) + list(items), axis=axis)
    return lax.dynamic_slice_in_dim(twice, (size - me) % size * width, size * width, axis=axis)


def tied(value, *after):
    return lax.optimization_barrier((value, after))[0]


def swap_parts(parts):
    size = len(parts)
    return [parts[0]] + [send_down(parts[size - k], k) for k in range(1, size)]


def swap_full(value):
    return [value] + [send_down(value, k) for k in range(1, lax.axis_size("img"))]


def other_rows(weight):
    size = lax.axis_size("img")
    tiles = lax.axis_size("row") * lax.axis_size("col")
    at = lax.axis_index("row") * lax.axis_size("col") + lax.axis_index("col")
    rows, width = weight.shape
    each = -(-rows // (tiles * 8)) * 8
    start = jnp.minimum(at * each, rows - each)
    piece = lax.dynamic_slice(weight, (start, 0), (each, width))
    if rows % each:
        lag = jnp.clip(at * each - start, 0, each)
        piece = lax.dynamic_slice(jnp.concatenate([piece, piece], 0), (lag, 0), (each, width))
    pieces = [send_down(piece, k) for k in range(1, size)]
    if size == 2:
        return [lax.all_gather(pieces[0], RC, axis=0, tiled=True)], pieces
    full = lax.all_gather(jnp.stack(pieces), RC, axis=1, tiled=True)
    return [full[k] for k in range(size - 1)], pieces


def widened(part, rows, axis):
    extra = rows - part.shape[axis]
    if extra == 0:
        return part
    pads = [(0, 0), (0, 0)]
    pads[axis] = (0, extra)
    return jnp.pad(part, pads)


def quad_order(rows_n, cols_n):
    def quad(s):
        return s // cols_n * 2 // rows_n * 2 + s % cols_n * 2 // cols_n

    return sorted(range(rows_n * cols_n), key=quad)


def pick_tokens(pieces, par, half):
    lane = lax.broadcasted_iota(jnp.int32, pieces[0].shape, 1)
    tiles = []
    for j in range(0, len(pieces), 2):
        a = pieces[j].astype(F32)
        b = pieces[j + 1].astype(F32)
        if par == 0:
            tile = jnp.where(lane < half, a, pltpu.roll(b, half, 1))
        else:
            tile = jnp.where(lane < half, pltpu.roll(a, half, 1), b)
        tiles.append(tile.astype(BF))
    return jnp.concatenate(tiles, axis=1)


def put_tokens(first, second, spot, half):
    tile = spot // 2
    a = first[:, tile * 2 * half : (tile + 1) * 2 * half]
    b = second[:, tile * 2 * half : (tile + 1) * 2 * half]
    lane = lax.broadcasted_iota(jnp.int32, a.shape, 1)
    if spot % 2 == 0:
        return jnp.where(lane < half, a, pltpu.roll(b, half, 1))
    return jnp.where(lane < half, pltpu.roll(a, half, 1), b)


def attend_kernel(order, half, factor, kind_ref, x_ref, o_ref, lse_ref, qkv_s, o_s):
    step = pl.program_id(1)
    count = len(order) * half
    block = count // 4
    coef = factor * math.log2(math.e)
    for par in range(2):
        for c in range(3):
            qkv_s[c] = pick_tokens([x_ref[s, 0, c] for s in order], par, half)
        single = kind_ref[2 * step + par] == 0
        for b in range(4):
            cols = slice(b * block, (b + 1) * block)

            def work(keys, cols=cols, par=par):
                query = qkv_s[0, :, cols]
                score = dotd(qkv_s[1, :, keys], query, 0, 0)
                top = jnp.max(score, axis=0, keepdims=True)
                expd = jnp.exp2((score - top) * coef)
                total = jnp.sum(expd, axis=0, keepdims=True)
                out = dotd(qkv_s[2, :, keys], expd.astype(BF), 1, 0)
                o_s[par, :, cols] = out * (1.0 / total)
                lse_ref[0, par, :, cols] = top * coef + jnp.log2(total)

            @pl.when(single)
            def _():
                work(slice(0, count))

            @pl.when(jnp.logical_not(single))
            def _():
                work(cols)

    for i, s in enumerate(order):
        o_ref[s, 0] = put_tokens(o_s[0], o_s[1], i, half).astype(BF)


def attend_back_kernel(
    order, half, factor, kind_ref, x_ref, d_ref, lse_ref, g_ref, qkv_s, d_s, g_s
):
    step = pl.program_id(1)
    count = len(order) * half
    block = count // 4
    coef = factor * math.log2(math.e)
    for par in range(2):
        for c in range(3):
            qkv_s[c] = pick_tokens([x_ref[s, 0, c] for s in order], par, half)
        d_s[...] = pick_tokens([d_ref[s, 0] for s in order], par, half)
        single = kind_ref[2 * step + par] == 0
        for b in range(4):
            cols = slice(b * block, (b + 1) * block)

            def work(keys, fresh, cols=cols, par=par):
                query = qkv_s[0, :, cols]
                dout = d_s[:, cols]
                score = dotd(qkv_s[1, :, keys], query, 0, 0)
                prob = jnp.exp2(score * coef - lse_ref[0, par, :, cols])
                dprob = dotd(qkv_s[2, :, keys], dout, 0, 0)
                delta = jnp.sum(prob * dprob, axis=0, keepdims=True)
                dscore = (prob * (dprob - delta)).astype(BF)
                g_s[par, 0, :, cols] = dotd(qkv_s[1, :, keys], dscore, 1, 0) * factor
                dkey = dotd(query, dscore, 1, 1) * factor
                dvalue = dotd(dout, prob.astype(BF), 1, 1)
                if fresh:
                    g_s[par, 1, :, keys] = dkey
                    g_s[par, 2, :, keys] = dvalue
                else:
                    g_s[par, 1, :, keys] += dkey
                    g_s[par, 2, :, keys] += dvalue

            @pl.when(single)
            def _():
                work(slice(0, count), b == 0)

            @pl.when(jnp.logical_not(single))
            def _():
                work(cols, True)

    for c in range(3):
        for i, s in enumerate(order):
            g_ref[s, 0, c] = put_tokens(g_s[0, c], g_s[1, c], i, half).astype(BF)


def attend(kinds, x, order, half, factor):
    tiles, per, _, depth, tokens = x.shape
    count = tiles * half
    pairs = tokens // (2 * half)
    return pl.pallas_call(
        lambda *refs: attend_kernel(order, half, factor, *refs),
        grid_spec=pltpu.PrefetchScalarGridSpec(
            num_scalar_prefetch=1,
            grid=(per, pairs),
            in_specs=[
                pl.BlockSpec((tiles, 1, 3, depth, 2 * half), lambda h, p, kd: (0, h, 0, 0, p))
            ],
            out_specs=[
                pl.BlockSpec((tiles, 1, depth, 2 * half), lambda h, p, kd: (0, h, 0, p)),
                pl.BlockSpec((1, 2, 1, count), lambda h, p, kd: (h, p, 0, 0)),
            ],
            scratch_shapes=[
                pltpu.VMEM((3, depth, count), BF),
                pltpu.VMEM((2, depth, count), F32),
            ],
        ),
        out_shape=[
            jax.ShapeDtypeStruct((tiles, per, depth, tokens), BF),
            jax.ShapeDtypeStruct((per, 2 * pairs, 1, count), F32),
        ],
        name="attend",
        cost_estimate=pl.CostEstimate(
            flops=10**10, bytes_accessed=4 * 10**7, transcendentals=per * tokens * count
        ),
    )(kinds, x)


def attend_back(kinds, x, d, lse, order, half, factor):
    tiles, per, _, depth, tokens = x.shape
    count = tiles * half
    pairs = tokens // (2 * half)
    return pl.pallas_call(
        lambda *refs: attend_back_kernel(order, half, factor, *refs),
        grid_spec=pltpu.PrefetchScalarGridSpec(
            num_scalar_prefetch=1,
            grid=(per, pairs),
            in_specs=[
                pl.BlockSpec((tiles, 1, 3, depth, 2 * half), lambda h, p, kd: (0, h, 0, 0, p)),
                pl.BlockSpec((tiles, 1, depth, 2 * half), lambda h, p, kd: (0, h, 0, p)),
                pl.BlockSpec((1, 2, 1, count), lambda h, p, kd: (h, p, 0, 0)),
            ],
            out_specs=pl.BlockSpec(
                (tiles, 1, 3, depth, 2 * half), lambda h, p, kd: (0, h, 0, 0, p)
            ),
            scratch_shapes=[
                pltpu.VMEM((3, depth, count), BF),
                pltpu.VMEM((depth, count), BF),
                pltpu.VMEM((2, 3, depth, count), F32),
            ],
        ),
        out_shape=jax.ShapeDtypeStruct(x.shape, BF),
        name="attend_back",
        cost_estimate=pl.CostEstimate(
            flops=10**10, bytes_accessed=4 * 10**7, transcendentals=per * tokens * count
        ),
    )(kinds, x, d, lse)


def swapped(value, axis, bit):
    return lax.ppermute(value, axis, [(j, j ^ bit) for j in range(lax.axis_size(axis))])


def added(a, b):
    return (a.astype(F32) + b.astype(F32)).astype(BF)


def halved(value, axis, bit):
    upper = lax.axis_index(axis) // bit % 2
    rows = value.shape[0] // 2
    keep = lax.dynamic_slice_in_dim(value, upper * rows, rows, 0)
    give = lax.dynamic_slice_in_dim(value, (1 - upper) * rows, rows, 0)
    return added(keep, swapped(give, axis, bit))


def doubled(value, axis, bit):
    upper = lax.axis_index(axis) // bit % 2
    got = swapped(value, axis, bit)
    return jnp.where(
        upper == 0, jnp.concatenate([value, got], 0), jnp.concatenate([got, value], 0)
    )


def bits_of(axis):
    return [(axis, 1 << i) for i in range(lax.axis_size(axis).bit_length() - 1)]


def tile_halved(value):
    bits = bits_of("row") + bits_of("col")
    for axis, bit in bits[:-1]:
        value = halved(value, axis, bit)
    axis, bit = bits[-1]
    return added(value, swapped(value, axis, bit))


def tile_doubled(value):
    bits = bits_of("row") + bits_of("col")
    for axis, bit in bits[-2::-1]:
        value = doubled(value, axis, bit)
    return value


def exchange(x):
    return lax.all_to_all(x, RC, split_axis=0, concat_axis=0, tiled=True)


def blank(shape, dtype):
    return pl.pallas_call(
        lambda ref: None,
        out_specs=pl.BlockSpec(memory_space=pl.ANY),
        out_shape=jax.ShapeDtypeStruct(shape, dtype),
        name="blank",
    )()


def summed_apart(small, items, finish):
    once = 1 + jnp.minimum(lax.axis_index("row"), 0)
    tiles, each, width = small.shape
    imgs = lax.axis_size("img")

    def body(_, state):
        parts = jnp.sum(exchange(state[0]).astype(F32), axis=0).astype(BF)
        parts = jnp.stack(swap_full(parts))
        parts = exchange(jnp.broadcast_to(parts[None], (tiles,) + parts.shape))
        parts = parts.transpose(1, 0, 2, 3)
        done = finish(parts.reshape(imgs, tiles * each, width))
        sums = [tile_halved(value) for value in state[1]]
        late = len(sums) // 2
        sums[late:], done = lax.optimization_barrier((sums[late:], done))
        return parts[0], [tile_doubled(value) for value in sums], done

    empty = jax.eval_shape(finish, jax.ShapeDtypeStruct((imgs, tiles * each, width), BF))
    empty = jax.tree.map(lambda item: blank(item.shape, item.dtype), empty)
    return lax.fori_loop(0, once, body, (small, items, empty))[1:]


def outer_kernel(left_ref, right_ref, out_ref):
    out_ref[...] = dotd(left_ref[...], right_ref[...], 0, 0)


def outer(left, right, block):
    depth, rows = left.shape
    cols = right.shape[1]
    return pl.pallas_call(
        outer_kernel,
        grid=(cols // block,),
        in_specs=[
            pl.BlockSpec((depth, rows), lambda j: (0, 0)),
            pl.BlockSpec((depth, block), lambda j: (0, j)),
        ],
        out_specs=pl.BlockSpec((rows, block), lambda j: (0, j)),
        out_shape=jax.ShapeDtypeStruct((rows, cols), F32),
        name="outer",
    )(left, right)


def local(
    latent,
    cotangent,
    cond,
    canvas_kind,
    w_patch,
    w_qkv,
    w_proj,
    w_up,
    w_down,
    w_ada,
    w_final_ada,
    w_out,
):
    local_n, chans, tile_r, tile_c = latent.shape
    out_ch = cotangent.shape[1]
    slots = cond.shape[1]
    width = cond.shape[2]
    inner = w_up.shape[1]
    imgs = lax.axis_size("img")
    rows_n = lax.axis_size("row")
    cols_n = lax.axis_size("col")
    row_at = lax.axis_index("row")
    col_at = lax.axis_index("col")
    tiles = rows_n * cols_n
    patch_r = tile_r // 2
    patch_c = tile_c // 2
    tile_tok = patch_r * patch_c
    half = patch_r * rows_n // 2
    half_c = patch_c * cols_n // 2
    head_dim = width // HEADS
    per = HEADS // tiles
    factor = head_dim ** (-0.5)
    rows = local_n * tile_tok
    order = quad_order(rows_n, cols_n)

    o_qkv, sent = other_rows(w_qkv)
    o_up, sent = other_rows(tied(w_up, sent))
    lower = w_down.shape[0] // 3
    w_straight = tied(w_down[:lower], sent)
    o_low = [send_down(w_straight, k) for k in range(1, imgs)]
    w_straight = tied(w_down[lower : 2 * lower], o_low)
    o_mid = [send_down(w_straight, k) for k in range(1, imgs)]
    wp = join_own([w_patch] + [send_down(w_patch, k) for k in range(1, imgs)], 0)
    wout = join_own([w_out] + [send_down(w_out, k) for k in range(1, imgs)], 0)

    stacked = jnp.concatenate([latent, cotangent], axis=1)
    upper = shifted(stacked[:, :, -1:, :], "row", 1)
    framed = jnp.concatenate([upper, stacked[:, :, :-1, :]], axis=2)
    beside = shifted(framed[:, :, :, -1:], "col", 1)
    framed = jnp.concatenate([beside, framed[:, :, :, :-1]], axis=3)

    def to_tokens(tile):
        depth = tile.shape[1]
        shaped = tile.reshape(local_n, depth, patch_r, 2, patch_c, 2).transpose(0, 2, 4, 1, 3, 5)
        return shaped.reshape(rows, depth * 4)

    def to_tile(tokens):
        depth = tokens.shape[1] // 4
        shaped = tokens.reshape(local_n, patch_r, patch_c, depth, 2, 2).transpose(0, 3, 1, 4, 2, 5)
        return shaped.reshape(local_n, depth, tile_r, tile_c)

    pieces = to_tokens(framed[:, :chans])
    dout = to_tokens(framed[:, chans:])

    quad = row_at * 2 // rows_n * 2 + col_at * 2 // cols_n
    slot = canvas_kind * quad
    picker = (slot[:, None] == jnp.arange(slots, dtype=jnp.int32)[None, :]).astype(F32)
    silu = swish(cond)
    silu_low = silu.astype(BF)
    chosen = jnp.sum(picker[:, :, None] * silu_low.astype(F32), axis=1).astype(BF)
    packed = jnp.concatenate([chosen, silu_low.reshape(local_n * slots, width)], axis=0)
    packed = swap_parts(split_own(packed, 1))
    silu_all = jnp.concatenate([item[local_n:] for item in packed], axis=0)
    chosen_all = jnp.concatenate([item[:local_n] for item in packed], axis=0)
    part = jnp.concatenate(
        [dotd(chosen_all, w_ada, 1, 0), dotd(chosen_all, w_final_ada, 1, 0)], axis=1
    )
    part = [part[k * local_n : (k + 1) * local_n] for k in range(imgs)]
    mods = part[0]
    for k in range(1, imgs):
        mods = mods + send_up(part[k], k)
    shift1, scale1, gate1, shift2, scale2, gate2, shiftf, scalef = jnp.split(mods, 8, axis=-1)

    prow = row_at * patch_r + jnp.arange(patch_r, dtype=jnp.int32)
    pcol = col_at * patch_c + jnp.arange(patch_c, dtype=jnp.int32)
    lrow = prow[None, :] - canvas_kind[:, None] * (prow[None, :] // half) * half
    lcol = pcol[None, :] - canvas_kind[:, None] * (pcol[None, :] // half_c) * half_c
    table_r = sincos(lrow, width // 4)
    table_c = sincos(lcol, width // 4)
    full = (local_n, patch_r, patch_c, width // 2)
    positions = jnp.concatenate(
        [
            jnp.broadcast_to(table_c[:, None, :, :], full),
            jnp.broadcast_to(table_r[:, :, None, :], full),
        ],
        axis=-1,
    ).reshape(local_n, tile_tok, width)

    def tokens3(value):
        return value.reshape(local_n, tile_tok, -1)

    x0 = tokens3(dotd(pieces, wp, 1, 0)) + positions
    a1 = modulate(x0, shift1, scale1).astype(BF).reshape(rows, width)
    o_proj, _ = other_rows(tied(w_proj, a1))
    o_high, _ = other_rows(tied(w_down[2 * lower :], a1))
    a1_parts = split_own(a1, 1)
    a1_all = jnp.concatenate(swap_parts(a1_parts), 0)

    def product(parts, own, others):
        total = dotd(parts[0], own, 1, 0)
        for part, other in zip(parts[1:], others):
            total = total + dotd(widened(part, other.shape[0], 1), other, 1, 0)
        return total

    def back_product(value, own, others):
        items = [dotd(value, own, 1, 1)]
        for other in others:
            items.append(dotd(value, other, 1, 1)[:, : own.shape[0]])
        return items

    qkv = dotd(w_qkv, a1_parts[0], 0, 1)
    for part, other in zip(a1_parts[1:], o_qkv):
        qkv = qkv + dotd(other, widened(part, other.shape[0], 1), 0, 1)
    qkv = qkv.astype(BF).reshape(3, tiles, per, head_dim, rows).transpose(1, 2, 0, 3, 4)
    qkv = exchange(qkv)
    qkv, o_low = lax.optimization_barrier((qkv, o_low))
    att, lse = attend(canvas_kind, qkv, order, tile_tok, factor)
    att = exchange(att).reshape(width, rows)
    att, a1_all, o_mid = lax.optimization_barrier((att, a1_all, o_mid))
    att_parts = split_own(att, 0)
    att_all = jnp.concatenate(swap_parts(att_parts), 1)
    proj = dotd(att_parts[0], w_proj, 0, 0)
    for part, other in zip(att_parts[1:], o_proj):
        proj = proj + dotd(widened(part, other.shape[0], 0), other, 0, 0)
    proj = tokens3(proj)
    x1 = x0 + gate1[:, None, :] * proj
    a2 = modulate(x1, shift2, scale2).astype(BF).reshape(rows, width)
    a2_parts = split_own(a2, 1)
    a2_all = jnp.concatenate(swap_parts(a2_parts), 0)
    pre = product(a2_parts, w_up, o_up)
    hid = gelu_tanh(pre).astype(BF)
    hid, att_all, a2_all = lax.optimization_barrier((hid, att_all, a2_all))
    hid_parts = split_own(hid, 1)
    hid_all = swap_parts(hid_parts)
    down = dotd(hid_parts[0], w_down, 1, 0)
    for part, low, mid, high in zip(hid_parts[1:], o_low, o_mid, o_high):
        straight = jnp.concatenate([low, mid], axis=0)
        down = down + dotd(part[:, : 2 * lower], straight, 1, 0)
        down = down + dotd(widened(part[:, 2 * lower :], high.shape[0], 1), high, 1, 0)
    down = tokens3(down)
    x2 = x1 + gate2[:, None, :] * down
    af = modulate(x2, shiftf, scalef).astype(BF).reshape(rows, width)
    outp = dotd(af, wout, 1, 0)

    g_out = dotd(dout, af, 0, 0)
    daf = tokens3(dotd(dout, wout, 1, 1))
    _, pull = jax.vjp(modulate, x2, shiftf, scalef)
    dx2, dshiftf, dscalef = pull(daf)
    dgate2 = jnp.sum(dx2 * down, axis=1)
    ddown = (gate2[:, None, :] * dx2).astype(BF).reshape(rows, width)
    ddown_all = swap_full(ddown)
    dhid = [dotd(ddown, w_down, 1, 1)]
    for low, mid, high in zip(o_low, o_mid, o_high):
        straight = jnp.concatenate([low, mid], axis=0)
        last = w_down.shape[0] - 2 * lower
        items = [dotd(ddown, straight, 1, 1), dotd(ddown, high, 1, 1)[:, :last]]
        dhid.append(jnp.concatenate(items, axis=1))
    dhid = join_own(dhid, 1)
    _, pull = jax.vjp(gelu_tanh, pre)
    dpre = pull(dhid)[0].astype(BF)
    dpre_all = swap_full(dpre)
    da2 = tokens3(join_own(back_product(dpre, w_up, o_up), 1))
    da2, hid_all, ddown_all = lax.optimization_barrier((da2, hid_all, ddown_all))
    g_down = dotd(jnp.concatenate(hid_all, 0), jnp.concatenate(ddown_all, 0), 0, 0).astype(BF)
    da2, g_down = lax.optimization_barrier((da2, g_down))
    g_down = lax.psum_scatter(g_down, RC, scatter_dimension=0, tiled=True)
    _, pull = jax.vjp(modulate, x1, shift2, scale2)
    dx1_norm, dshift2, dscale2 = pull(da2)
    dx1 = dx2 + dx1_norm
    dgate1 = jnp.sum(dx1 * proj, axis=1)
    dproj = (gate1[:, None, :] * dx1).astype(BF).reshape(rows, width)
    datt = [dotd(w_proj, dproj, 1, 1)]
    for other in o_proj:
        datt.append(dotd(other, dproj, 1, 1)[: w_proj.shape[0]])
    datt = join_own(datt, 0).astype(BF)
    datt = exchange(datt.reshape(tiles, per, head_dim, rows))
    dproj_all = jnp.concatenate(swap_full(dproj), 0)
    dqkv = attend_back(canvas_kind, qkv, datt, lse, order, tile_tok, factor)
    dqkv, dpre_all = lax.optimization_barrier((dqkv, dpre_all))
    dqkv = exchange(dqkv)
    g_up = dotd(a2_all, jnp.concatenate(dpre_all, 0), 0, 0).astype(BF)
    g_proj = dotd(att_all, dproj_all, 1, 0).astype(BF)
    dqkv, g_up, g_down, g_proj, outp, g_out = lax.optimization_barrier(
        (dqkv, g_up, g_down, g_proj, outp, g_out)
    )
    g_down = lax.all_gather(g_down, RC, axis=0, tiled=True)
    dqkv = dqkv.transpose(2, 0, 1, 3, 4).reshape(3 * width, rows)
    dqkv_all = jnp.concatenate(swap_full(dqkv), 1)
    dqkv_all, g_up, g_down = lax.optimization_barrier((dqkv_all, g_up, g_down))
    g_up = lax.psum(g_up, RC)
    da1 = [dotd(dqkv, w_qkv, 0, 1)]
    for other in o_qkv:
        da1.append(dotd(dqkv, other, 0, 1)[:, : w_qkv.shape[0]])
    da1 = tokens3(join_own(da1, 1))
    g_att = [
        dotd(a1_all, dqkv_all[c * width : (c + 1) * width], 0, 1).astype(BF) for c in range(3)
    ]
    _, pull = jax.vjp(modulate, x0, shift1, scale1)
    dx0_norm, dshift1, dscale1 = pull(da1)
    dtok = (dx1 + dx0_norm).astype(BF).reshape(rows, width)
    g_patch = dotd(pieces, dtok, 0, 0)
    dpatch = dotd(dtok, wp, 1, 1)

    dmods = jnp.concatenate(
        [dshift1, dscale1, dgate1, dshift2, dscale2, dgate2, dshiftf, dscalef], axis=-1
    )
    dmods = (picker[:, :, None] * dmods[:, None, :]).reshape(local_n * slots * 8, width)
    small = jnp.concatenate([g_patch, g_out, dmods], axis=0)
    n_patch = g_patch.shape[0]
    n_out = g_out.shape[0]
    count = small.shape[0]
    each = -(-count // tiles)
    small = jnp.pad(small, ((0, each * tiles - count), (0, 0))).astype(BF)
    step = local_n * slots

    def split_small(value):
        return value[:, n_patch + n_out : count].reshape(imgs * step, 8 * width)

    def finish(value):
        sums = jnp.sum(value[:, : n_patch + n_out].astype(F32), axis=0)
        dmods = split_small(value)
        dsilu = dotd(dmods[:, : 6 * width], w_ada, 1, 1)
        dsilu = dsilu + dotd(dmods[:, 6 * width :], w_final_ada, 1, 1)
        dsilu = [dsilu[k * step : (k + 1) * step] for k in range(imgs)]
        dsilu = [dsilu[0]] + [send_up(dsilu[imgs - k], imgs - k) for k in range(1, imgs)]
        return (
            sums,
            join_own(dsilu, 1),
            outer(silu_all, dmods[:, : 6 * width], width),
            outer(silu_all, dmods[:, 6 * width :], width),
            g_down.astype(F32),
        )

    g_att, done = summed_apart(small.reshape(tiles, each, width), g_att + [g_proj], finish)
    sums, dsilu, g_ada, g_fada, g_down = done
    g_qkv = jnp.concatenate(g_att[:3], axis=1)
    g_proj = g_att[3]
    g_patch = split_own(sums[:n_patch], 0)[0]
    g_out = split_own(sums[n_patch:], 1)[0].T
    dsilu = dsilu.reshape(local_n, slots, width)
    _, pull = jax.vjp(swish, cond)
    cond_grad = pull(dsilu)[0]

    joined = jnp.concatenate([to_tile(outp), to_tile(dpatch)], axis=1)
    right_rim = shifted(joined[:, :, :, :1], "col", -1)
    joined = jnp.concatenate([joined[:, :, :, 1:], right_rim], axis=3)
    lower_rim = shifted(joined[:, :, :1, :], "row", -1)
    joined = jnp.concatenate([joined[:, :, 1:, :], lower_rim], axis=2)
    return (
        joined[:, :out_ch],
        joined[:, out_ch:],
        cond_grad,
        g_patch,
        g_qkv.astype(F32),
        g_proj.astype(F32),
        g_up.astype(F32),
        g_down,
        g_ada,
        g_fada,
        g_out,
    )


def solution(mesh):
    rows = P("img", None)
    tile = P("img", None, "row", "col")
    whole = P("img", None, None)
    return jax.shard_map(
        local,
        mesh=mesh,
        in_specs=(tile, tile, whole, P("img")) + (rows,) * 8,
        out_specs=(tile, tile, whole) + (rows,) * 8,
        check_vma=False,
    )
```

```python
import math

import jax
import jax.numpy as jnp
from jax import lax
from jax.experimental import pallas as pl
from jax.experimental.pallas import tpu as pltpu
from jax.sharding import PartitionSpec as P

HEADS = 16
RC = ("row", "col")
BF = jnp.bfloat16
F32 = jnp.float32


def shifted(block, axis, distance):
    size = lax.axis_size(axis)
    return lax.ppermute(block, axis, [((i - distance) % size, i) for i in range(size)])


def layer_norm(value):
    center = value - jnp.mean(value, -1, keepdims=True)
    spread = jnp.mean(center * center, -1, keepdims=True)
    return center * lax.rsqrt(spread + 1e-06)


def modulate(value, shift, scale):
    return layer_norm(value) * (1.0 + scale[:, None, :]) + shift[:, None, :]


def gelu_tanh(value):
    return jax.nn.gelu(value, approximate=True)


def swish(value):
    return value * jax.nn.sigmoid(value)


def sincos(coord, count):
    freqs = 1.0 / 10000.0 ** (jnp.arange(count, dtype=F32) / count)
    angle = coord.astype(F32)[..., None] * freqs
    return jnp.concatenate([jnp.sin(angle), jnp.cos(angle)], axis=-1)


def dotd(left, right, ldim, rdim):
    return lax.dot_general(
        left, right, (((ldim,), (rdim,)), ((), ())), preferred_element_type=F32
    )


def send_down(value, k):
    size = lax.axis_size("img")
    return lax.ppermute(value, "img", [(j, (j - k) % size) for j in range(size)])


def send_up(value, k):
    size = lax.axis_size("img")
    return lax.ppermute(value, "img", [(j, (j + k) % size) for j in range(size)])


def split_own(value, axis):
    size = lax.axis_size("img")
    me = lax.axis_index("img")
    width = value.shape[axis] // size
    blocks = [lax.slice_in_dim(value, i * width, (i + 1) * width, axis=axis) for i in range(size)]
    if size == 2:
        return [
            jnp.where(me == 0, blocks[0], blocks[1]),
            jnp.where(me == 0, blocks[1], blocks[0]),
        ]
    return [
        lax.dynamic_slice_in_dim(value, (me + k) % size * width, width, axis=axis)
        for k in range(size)
    ]


def join_own(items, axis):
    size = lax.axis_size("img")
    me = lax.axis_index("img")
    if size == 2:
        return jnp.concatenate(
            [jnp.where(me == 0, items[0], items[1]), jnp.where(me == 0, items[1], items[0])],
            axis=axis,
        )
    width = items[0].shape[axis]
    twice = jnp.concatenate(list(items) + list(items), axis=axis)
    return lax.dynamic_slice_in_dim(twice, (size - me) % size * width, size * width, axis=axis)


def tied(value, *after):
    return lax.optimization_barrier((value, after))[0]


def swap_parts(parts):
    size = len(parts)
    return [parts[0]] + [send_down(parts[size - k], k) for k in range(1, size)]


def swap_full(value):
    return [value] + [send_down(value, k) for k in range(1, lax.axis_size("img"))]


def other_rows(weight):
    size = lax.axis_size("img")
    tiles = lax.axis_size("row") * lax.axis_size("col")
    at = lax.axis_index("row") * lax.axis_size("col") + lax.axis_index("col")
    rows, width = weight.shape
    each = -(-rows // (tiles * 8)) * 8
    start = jnp.minimum(at * each, rows - each)
    piece = lax.dynamic_slice(weight, (start, 0), (each, width))
    if rows % each:
        lag = jnp.clip(at * each - start, 0, each)
        piece = lax.dynamic_slice(jnp.concatenate([piece, piece], 0), (lag, 0), (each, width))
    pieces = [send_down(piece, k) for k in range(1, size)]
    if size == 2:
        return [lax.all_gather(pieces[0], RC, axis=0, tiled=True)], pieces
    full = lax.all_gather(jnp.stack(pieces), RC, axis=1, tiled=True)
    return [full[k] for k in range(size - 1)], pieces


def widened(part, rows, axis):
    extra = rows - part.shape[axis]
    if extra == 0:
        return part
    pads = [(0, 0), (0, 0)]
    pads[axis] = (0, extra)
    return jnp.pad(part, pads)


def quad_order(rows_n, cols_n):
    def quad(s):
        return s // cols_n * 2 // rows_n * 2 + s % cols_n * 2 // cols_n

    return sorted(range(rows_n * cols_n), key=quad)


def pick_tokens(pieces, par, half):
    lane = lax.broadcasted_iota(jnp.int32, pieces[0].shape, 1)
    tiles = []
    for j in range(0, len(pieces), 2):
        a = pieces[j].astype(F32)
        b = pieces[j + 1].astype(F32)
        if par == 0:
            tile = jnp.where(lane < half, a, pltpu.roll(b, half, 1))
        else:
            tile = jnp.where(lane < half, pltpu.roll(a, half, 1), b)
        tiles.append(tile.astype(BF))
    return jnp.concatenate(tiles, axis=1)


def put_tokens(first, second, spot, half):
    tile = spot // 2
    a = first[:, tile * 2 * half : (tile + 1) * 2 * half]
    b = second[:, tile * 2 * half : (tile + 1) * 2 * half]
    lane = lax.broadcasted_iota(jnp.int32, a.shape, 1)
    if spot % 2 == 0:
        return jnp.where(lane < half, a, pltpu.roll(b, half, 1))
    return jnp.where(lane < half, pltpu.roll(a, half, 1), b)


def attend_kernel(order, half, factor, kind_ref, x_ref, o_ref, lse_ref, qkv_s, o_s):
    step = pl.program_id(1)
    count = len(order) * half
    block = count // 4
    coef = factor * math.log2(math.e)
    for par in range(2):
        for c in range(3):
            qkv_s[c] = pick_tokens([x_ref[s, 0, c] for s in order], par, half)
        single = kind_ref[2 * step + par] == 0
        for b in range(4):
            cols = slice(b * block, (b + 1) * block)

            def work(keys, cols=cols, par=par):
                query = qkv_s[0, :, cols]
                score = dotd(qkv_s[1, :, keys], query, 0, 0)
                top = jnp.max(score, axis=0, keepdims=True)
                expd = jnp.exp2((score - top) * coef)
                total = jnp.sum(expd, axis=0, keepdims=True)
                out = dotd(qkv_s[2, :, keys], expd.astype(BF), 1, 0)
                o_s[par, :, cols] = out * (1.0 / total)
                lse_ref[0, par, :, cols] = top * coef + jnp.log2(total)

            @pl.when(single)
            def _():
                work(slice(0, count))

            @pl.when(jnp.logical_not(single))
            def _():
                work(cols)

    for i, s in enumerate(order):
        o_ref[s, 0] = put_tokens(o_s[0], o_s[1], i, half).astype(BF)


def attend_back_kernel(
    order, half, factor, kind_ref, x_ref, d_ref, o_ref, lse_ref, g_ref, qkv_s, d_s, e_s, g_s
):
    step = pl.program_id(1)
    count = len(order) * half
    block = count // 4
    coef = factor * math.log2(math.e)
    for par in range(2):
        for c in range(3):
            qkv_s[c] = pick_tokens([x_ref[s, 0, c] for s in order], par, half)
        dout_all = pick_tokens([d_ref[s, 0] for s in order], par, half)
        out_all = pick_tokens([o_ref[s, 0] for s in order], par, half)
        d_s[...] = dout_all
        e_s[...] = jnp.sum(dout_all.astype(F32) * out_all.astype(F32), axis=0, keepdims=True)
        single = kind_ref[2 * step + par] == 0
        for b in range(4):
            cols = slice(b * block, (b + 1) * block)

            def work(keys, fresh, cols=cols, par=par):
                query = qkv_s[0, :, cols]
                dout = d_s[:, cols]
                score = dotd(qkv_s[1, :, keys], query, 0, 0)
                prob = jnp.exp2(score * coef - lse_ref[0, par, :, cols])
                dprob = dotd(qkv_s[2, :, keys], dout, 0, 0)
                dscore = (prob * (dprob - e_s[:, cols])).astype(BF)
                g_s[par, 0, :, cols] = dotd(qkv_s[1, :, keys], dscore, 1, 0) * factor
                dkey = dotd(query, dscore, 1, 1) * factor
                dvalue = dotd(dout, prob.astype(BF), 1, 1)
                if fresh:
                    g_s[par, 1, :, keys] = dkey
                    g_s[par, 2, :, keys] = dvalue
                else:
                    g_s[par, 1, :, keys] += dkey
                    g_s[par, 2, :, keys] += dvalue

            @pl.when(single)
            def _():
                work(slice(0, count), b == 0)

            @pl.when(jnp.logical_not(single))
            def _():
                work(cols, True)

    for c in range(3):
        for i, s in enumerate(order):
            g_ref[s, 0, c] = put_tokens(g_s[0, c], g_s[1, c], i, half).astype(BF)


def attend(kinds, x, order, half, factor):
    tiles, per, _, depth, tokens = x.shape
    count = tiles * half
    pairs = tokens // (2 * half)
    return pl.pallas_call(
        lambda *refs: attend_kernel(order, half, factor, *refs),
        grid_spec=pltpu.PrefetchScalarGridSpec(
            num_scalar_prefetch=1,
            grid=(per, pairs),
            in_specs=[
                pl.BlockSpec((tiles, 1, 3, depth, 2 * half), lambda h, p, kd: (0, h, 0, 0, p))
            ],
            out_specs=[
                pl.BlockSpec((tiles, 1, depth, 2 * half), lambda h, p, kd: (0, h, 0, p)),
                pl.BlockSpec((1, 2, 1, count), lambda h, p, kd: (h, p, 0, 0)),
            ],
            scratch_shapes=[
                pltpu.VMEM((3, depth, count), BF),
                pltpu.VMEM((2, depth, count), F32),
            ],
        ),
        out_shape=[
            jax.ShapeDtypeStruct((tiles, per, depth, tokens), BF),
            jax.ShapeDtypeStruct((per, 2 * pairs, 1, count), F32),
        ],
        name="attend",
        cost_estimate=pl.CostEstimate(
            flops=10**10, bytes_accessed=4 * 10**7, transcendentals=per * tokens * count
        ),
    )(kinds, x)


def attend_back(kinds, x, d, o, lse, order, half, factor):
    tiles, per, _, depth, tokens = x.shape
    count = tiles * half
    pairs = tokens // (2 * half)
    return pl.pallas_call(
        lambda *refs: attend_back_kernel(order, half, factor, *refs),
        grid_spec=pltpu.PrefetchScalarGridSpec(
            num_scalar_prefetch=1,
            grid=(per, pairs),
            in_specs=[
                pl.BlockSpec((tiles, 1, 3, depth, 2 * half), lambda h, p, kd: (0, h, 0, 0, p)),
                pl.BlockSpec((tiles, 1, depth, 2 * half), lambda h, p, kd: (0, h, 0, p)),
                pl.BlockSpec((tiles, 1, depth, 2 * half), lambda h, p, kd: (0, h, 0, p)),
                pl.BlockSpec((1, 2, 1, count), lambda h, p, kd: (h, p, 0, 0)),
            ],
            out_specs=pl.BlockSpec(
                (tiles, 1, 3, depth, 2 * half), lambda h, p, kd: (0, h, 0, 0, p)
            ),
            scratch_shapes=[
                pltpu.VMEM((3, depth, count), BF),
                pltpu.VMEM((depth, count), BF),
                pltpu.VMEM((1, count), F32),
                pltpu.VMEM((2, 3, depth, count), F32),
            ],
        ),
        out_shape=jax.ShapeDtypeStruct(x.shape, BF),
        name="attend_back",
        cost_estimate=pl.CostEstimate(
            flops=10**10, bytes_accessed=4 * 10**7, transcendentals=per * tokens * count
        ),
    )(kinds, x, d, o, lse)


def swapped(value, axis, bit):
    return lax.ppermute(value, axis, [(j, j ^ bit) for j in range(lax.axis_size(axis))])


def added(a, b):
    return (a.astype(F32) + b.astype(F32)).astype(BF)


def halved(value, axis, bit):
    upper = lax.axis_index(axis) // bit % 2
    rows = value.shape[0] // 2
    keep = lax.dynamic_slice_in_dim(value, upper * rows, rows, 0)
    give = lax.dynamic_slice_in_dim(value, (1 - upper) * rows, rows, 0)
    return added(keep, swapped(give, axis, bit))


def doubled(value, axis, bit):
    upper = lax.axis_index(axis) // bit % 2
    got = swapped(value, axis, bit)
    return jnp.where(
        upper == 0, jnp.concatenate([value, got], 0), jnp.concatenate([got, value], 0)
    )


def bits_of(axis):
    return [(axis, 1 << i) for i in range(lax.axis_size(axis).bit_length() - 1)]


def tile_halved(value):
    bits = bits_of("row") + bits_of("col")
    for axis, bit in bits[:-1]:
        value = halved(value, axis, bit)
    axis, bit = bits[-1]
    return added(value, swapped(value, axis, bit))


def tile_doubled(value):
    bits = bits_of("row") + bits_of("col")
    for axis, bit in bits[-2::-1]:
        value = doubled(value, axis, bit)
    return value


def exchange(x):
    return lax.all_to_all(x, RC, split_axis=0, concat_axis=0, tiled=True)


def blank(shape, dtype):
    return pl.pallas_call(
        lambda ref: None,
        out_specs=pl.BlockSpec(memory_space=pl.ANY),
        out_shape=jax.ShapeDtypeStruct(shape, dtype),
        name="blank",
    )()


def summed_apart(small, items, finish):
    once = 1 + jnp.minimum(lax.axis_index("row"), 0)
    tiles, each, width = small.shape
    imgs = lax.axis_size("img")

    def body(_, state):
        parts = jnp.sum(exchange(state[0]).astype(F32), axis=0).astype(BF)
        parts = jnp.stack(swap_full(parts))
        parts = exchange(jnp.broadcast_to(parts[None], (tiles,) + parts.shape))
        parts = parts.transpose(1, 0, 2, 3)
        done = finish(parts.reshape(imgs, tiles * each, width))
        sums = [tile_halved(value) for value in state[1]]
        late = len(sums) // 2
        sums[late:], done = lax.optimization_barrier((sums[late:], done))
        return parts[0], [tile_doubled(value) for value in sums], done

    empty = jax.eval_shape(finish, jax.ShapeDtypeStruct((imgs, tiles * each, width), BF))
    empty = jax.tree.map(lambda item: blank(item.shape, item.dtype), empty)
    return lax.fori_loop(0, once, body, (small, items, empty))[1:]


def outer_kernel(left_ref, right_ref, out_ref):
    out_ref[...] = dotd(left_ref[...], right_ref[...], 0, 0)


def outer(left, right, block):
    depth, rows = left.shape
    cols = right.shape[1]
    return pl.pallas_call(
        outer_kernel,
        grid=(cols // block,),
        in_specs=[
            pl.BlockSpec((depth, rows), lambda j: (0, 0)),
            pl.BlockSpec((depth, block), lambda j: (0, j)),
        ],
        out_specs=pl.BlockSpec((rows, block), lambda j: (0, j)),
        out_shape=jax.ShapeDtypeStruct((rows, cols), F32),
        name="outer",
    )(left, right)


def local(
    latent,
    cotangent,
    cond,
    canvas_kind,
    w_patch,
    w_qkv,
    w_proj,
    w_up,
    w_down,
    w_ada,
    w_final_ada,
    w_out,
):
    local_n, chans, tile_r, tile_c = latent.shape
    out_ch = cotangent.shape[1]
    slots = cond.shape[1]
    width = cond.shape[2]
    inner = w_up.shape[1]
    imgs = lax.axis_size("img")
    rows_n = lax.axis_size("row")
    cols_n = lax.axis_size("col")
    row_at = lax.axis_index("row")
    col_at = lax.axis_index("col")
    tiles = rows_n * cols_n
    patch_r = tile_r // 2
    patch_c = tile_c // 2
    tile_tok = patch_r * patch_c
    half = patch_r * rows_n // 2
    half_c = patch_c * cols_n // 2
    head_dim = width // HEADS
    per = HEADS // tiles
    factor = head_dim ** (-0.5)
    rows = local_n * tile_tok
    order = quad_order(rows_n, cols_n)

    o_qkv, sent = other_rows(w_qkv)
    o_up, sent = other_rows(tied(w_up, sent))
    lower = w_down.shape[0] // 3
    w_straight = tied(w_down[:lower], sent)
    o_low = [send_down(w_straight, k) for k in range(1, imgs)]
    w_straight = tied(w_down[lower : 2 * lower], o_low)
    o_mid = [send_down(w_straight, k) for k in range(1, imgs)]
    wp = join_own([w_patch] + [send_down(w_patch, k) for k in range(1, imgs)], 0)
    wout = join_own([w_out] + [send_down(w_out, k) for k in range(1, imgs)], 0)

    stacked = jnp.concatenate([latent, cotangent], axis=1)
    upper = shifted(stacked[:, :, -1:, :], "row", 1)
    framed = jnp.concatenate([upper, stacked[:, :, :-1, :]], axis=2)
    beside = shifted(framed[:, :, :, -1:], "col", 1)
    framed = jnp.concatenate([beside, framed[:, :, :, :-1]], axis=3)

    def to_tokens(tile):
        depth = tile.shape[1]
        shaped = tile.reshape(local_n, depth, patch_r, 2, patch_c, 2).transpose(0, 2, 4, 1, 3, 5)
        return shaped.reshape(rows, depth * 4)

    def to_tile(tokens):
        depth = tokens.shape[1] // 4
        shaped = tokens.reshape(local_n, patch_r, patch_c, depth, 2, 2).transpose(0, 3, 1, 4, 2, 5)
        return shaped.reshape(local_n, depth, tile_r, tile_c)

    pieces = to_tokens(framed[:, :chans])
    dout = to_tokens(framed[:, chans:])

    quad = row_at * 2 // rows_n * 2 + col_at * 2 // cols_n
    slot = canvas_kind * quad
    picker = (slot[:, None] == jnp.arange(slots, dtype=jnp.int32)[None, :]).astype(F32)
    silu = swish(cond)
    silu_low = silu.astype(BF)
    chosen = jnp.sum(picker[:, :, None] * silu_low.astype(F32), axis=1).astype(BF)
    packed = jnp.concatenate([chosen, silu_low.reshape(local_n * slots, width)], axis=0)
    packed = swap_parts(split_own(packed, 1))
    silu_all = jnp.concatenate([item[local_n:] for item in packed], axis=0)
    chosen_all = jnp.concatenate([item[:local_n] for item in packed], axis=0)
    part = jnp.concatenate(
        [dotd(chosen_all, w_ada, 1, 0), dotd(chosen_all, w_final_ada, 1, 0)], axis=1
    )
    part = [part[k * local_n : (k + 1) * local_n] for k in range(imgs)]
    mods = part[0]
    for k in range(1, imgs):
        mods = mods + send_up(part[k], k)
    shift1, scale1, gate1, shift2, scale2, gate2, shiftf, scalef = jnp.split(mods, 8, axis=-1)

    prow = row_at * patch_r + jnp.arange(patch_r, dtype=jnp.int32)
    pcol = col_at * patch_c + jnp.arange(patch_c, dtype=jnp.int32)
    lrow = prow[None, :] - canvas_kind[:, None] * (prow[None, :] // half) * half
    lcol = pcol[None, :] - canvas_kind[:, None] * (pcol[None, :] // half_c) * half_c
    table_r = sincos(lrow, width // 4)
    table_c = sincos(lcol, width // 4)
    full = (local_n, patch_r, patch_c, width // 2)
    positions = jnp.concatenate(
        [
            jnp.broadcast_to(table_c[:, None, :, :], full),
            jnp.broadcast_to(table_r[:, :, None, :], full),
        ],
        axis=-1,
    ).reshape(local_n, tile_tok, width)

    def tokens3(value):
        return value.reshape(local_n, tile_tok, -1)

    x0 = tokens3(dotd(pieces, wp, 1, 0)) + positions
    a1 = modulate(x0, shift1, scale1).astype(BF).reshape(rows, width)
    o_proj, _ = other_rows(tied(w_proj, a1))
    o_high, _ = other_rows(tied(w_down[2 * lower :], a1))
    a1_parts = split_own(a1, 1)
    a1_all = jnp.concatenate(swap_parts(a1_parts), 0)

    def product(parts, own, others):
        total = dotd(parts[0], own, 1, 0)
        for part, other in zip(parts[1:], others):
            total = total + dotd(widened(part, other.shape[0], 1), other, 1, 0)
        return total

    def back_product(value, own, others):
        items = [dotd(value, own, 1, 1)]
        for other in others:
            items.append(dotd(value, other, 1, 1)[:, : own.shape[0]])
        return items

    qkv = dotd(w_qkv, a1_parts[0], 0, 1)
    for part, other in zip(a1_parts[1:], o_qkv):
        qkv = qkv + dotd(other, widened(part, other.shape[0], 1), 0, 1)
    qkv = qkv.astype(BF).reshape(3, tiles, per, head_dim, rows).transpose(1, 2, 0, 3, 4)
    qkv = exchange(qkv)
    qkv, o_low = lax.optimization_barrier((qkv, o_low))
    att, lse = attend(canvas_kind, qkv, order, tile_tok, factor)
    att_head = att
    att = exchange(att).reshape(width, rows)
    att, a1_all, o_mid = lax.optimization_barrier((att, a1_all, o_mid))
    att_parts = split_own(att, 0)
    att_all = jnp.concatenate(swap_parts(att_parts), 1)
    proj = dotd(att_parts[0], w_proj, 0, 0)
    for part, other in zip(att_parts[1:], o_proj):
        proj = proj + dotd(widened(part, other.shape[0], 0), other, 0, 0)
    proj = tokens3(proj)
    x1 = x0 + gate1[:, None, :] * proj
    a2 = modulate(x1, shift2, scale2).astype(BF).reshape(rows, width)
    a2_parts = split_own(a2, 1)
    a2_all = jnp.concatenate(swap_parts(a2_parts), 0)
    pre = product(a2_parts, w_up, o_up)
    hid = gelu_tanh(pre).astype(BF)
    hid, att_all, a2_all = lax.optimization_barrier((hid, att_all, a2_all))
    hid_parts = split_own(hid, 1)
    hid_all = swap_parts(hid_parts)
    down = dotd(hid_parts[0], w_down, 1, 0)
    for part, low, mid, high in zip(hid_parts[1:], o_low, o_mid, o_high):
        straight = jnp.concatenate([low, mid], axis=0)
        down = down + dotd(part[:, : 2 * lower], straight, 1, 0)
        down = down + dotd(widened(part[:, 2 * lower :], high.shape[0], 1), high, 1, 0)
    down = tokens3(down)
    x2 = x1 + gate2[:, None, :] * down
    af = modulate(x2, shiftf, scalef).astype(BF).reshape(rows, width)
    outp = dotd(af, wout, 1, 0)

    g_out = dotd(dout, af, 0, 0)
    daf = tokens3(dotd(dout, wout, 1, 1))
    _, pull = jax.vjp(modulate, x2, shiftf, scalef)
    dx2, dshiftf, dscalef = pull(daf)
    dgate2 = jnp.sum(dx2 * down, axis=1)
    ddown = (gate2[:, None, :] * dx2).astype(BF).reshape(rows, width)
    ddown_all = swap_full(ddown)
    dhid = [dotd(ddown, w_down, 1, 1)]
    for low, mid, high in zip(o_low, o_mid, o_high):
        straight = jnp.concatenate([low, mid], axis=0)
        last = w_down.shape[0] - 2 * lower
        items = [dotd(ddown, straight, 1, 1), dotd(ddown, high, 1, 1)[:, :last]]
        dhid.append(jnp.concatenate(items, axis=1))
    dhid = join_own(dhid, 1)
    _, pull = jax.vjp(gelu_tanh, pre)
    dpre = pull(dhid)[0].astype(BF)
    dpre_all = swap_full(dpre)
    da2 = tokens3(join_own(back_product(dpre, w_up, o_up), 1))
    da2, hid_all, ddown_all = lax.optimization_barrier((da2, hid_all, ddown_all))
    g_down = dotd(jnp.concatenate(hid_all, 0), jnp.concatenate(ddown_all, 0), 0, 0).astype(BF)
    da2, g_down = lax.optimization_barrier((da2, g_down))
    g_down = lax.psum_scatter(g_down, RC, scatter_dimension=0, tiled=True)
    _, pull = jax.vjp(modulate, x1, shift2, scale2)
    dx1_norm, dshift2, dscale2 = pull(da2)
    dx1 = dx2 + dx1_norm
    dgate1 = jnp.sum(dx1 * proj, axis=1)
    dproj = (gate1[:, None, :] * dx1).astype(BF).reshape(rows, width)
    datt = [dotd(w_proj, dproj, 1, 1)]
    for other in o_proj:
        datt.append(dotd(other, dproj, 1, 1)[: w_proj.shape[0]])
    datt = join_own(datt, 0).astype(BF)
    datt = exchange(datt.reshape(tiles, per, head_dim, rows))
    dproj_all = jnp.concatenate(swap_full(dproj), 0)
    dqkv = attend_back(canvas_kind, qkv, datt, att_head, lse, order, tile_tok, factor)
    dqkv, dpre_all = lax.optimization_barrier((dqkv, dpre_all))
    dqkv = exchange(dqkv)
    g_up = dotd(a2_all, jnp.concatenate(dpre_all, 0), 0, 0).astype(BF)
    g_proj = dotd(att_all, dproj_all, 1, 0).astype(BF)
    dqkv, g_up, g_down, g_proj, outp, g_out = lax.optimization_barrier(
        (dqkv, g_up, g_down, g_proj, outp, g_out)
    )
    g_down = lax.all_gather(g_down, RC, axis=0, tiled=True)
    dqkv = dqkv.transpose(2, 0, 1, 3, 4).reshape(3 * width, rows)
    dqkv_all = jnp.concatenate(swap_full(dqkv), 1)
    dqkv_all, g_up, g_down = lax.optimization_barrier((dqkv_all, g_up, g_down))
    g_up = lax.psum(g_up, RC)
    da1 = [dotd(dqkv, w_qkv, 0, 1)]
    for other in o_qkv:
        da1.append(dotd(dqkv, other, 0, 1)[:, : w_qkv.shape[0]])
    da1 = tokens3(join_own(da1, 1))
    g_att = [
        dotd(a1_all, dqkv_all[c * width : (c + 1) * width], 0, 1).astype(BF) for c in range(3)
    ]
    _, pull = jax.vjp(modulate, x0, shift1, scale1)
    dx0_norm, dshift1, dscale1 = pull(da1)
    dtok = (dx1 + dx0_norm).astype(BF).reshape(rows, width)
    g_patch = dotd(pieces, dtok, 0, 0)
    dpatch = dotd(dtok, wp, 1, 1)

    dmods = jnp.concatenate(
        [dshift1, dscale1, dgate1, dshift2, dscale2, dgate2, dshiftf, dscalef], axis=-1
    )
    dmods = (picker[:, :, None] * dmods[:, None, :]).reshape(local_n * slots * 8, width)
    small = jnp.concatenate([g_patch, g_out, dmods], axis=0)
    n_patch = g_patch.shape[0]
    n_out = g_out.shape[0]
    count = small.shape[0]
    each = -(-count // tiles)
    small = jnp.pad(small, ((0, each * tiles - count), (0, 0))).astype(BF)
    step = local_n * slots

    def split_small(value):
        return value[:, n_patch + n_out : count].reshape(imgs * step, 8 * width)

    def finish(value):
        sums = jnp.sum(value[:, : n_patch + n_out].astype(F32), axis=0)
        dmods = split_small(value)
        dsilu = dotd(dmods[:, : 6 * width], w_ada, 1, 1)
        dsilu = dsilu + dotd(dmods[:, 6 * width :], w_final_ada, 1, 1)
        dsilu = [dsilu[k * step : (k + 1) * step] for k in range(imgs)]
        dsilu = [dsilu[0]] + [send_up(dsilu[imgs - k], imgs - k) for k in range(1, imgs)]
        return (
            sums,
            join_own(dsilu, 1),
            outer(silu_all, dmods[:, : 6 * width], width),
            outer(silu_all, dmods[:, 6 * width :], width),
            g_down.astype(F32),
        )

    g_att, done = summed_apart(small.reshape(tiles, each, width), g_att + [g_proj], finish)
    sums, dsilu, g_ada, g_fada, g_down = done
    g_qkv = jnp.concatenate(g_att[:3], axis=1)
    g_proj = g_att[3]
    g_patch = split_own(sums[:n_patch], 0)[0]
    g_out = split_own(sums[n_patch:], 1)[0].T
    dsilu = dsilu.reshape(local_n, slots, width)
    _, pull = jax.vjp(swish, cond)
    cond_grad = pull(dsilu)[0]

    joined = jnp.concatenate([to_tile(outp), to_tile(dpatch)], axis=1)
    right_rim = shifted(joined[:, :, :, :1], "col", -1)
    joined = jnp.concatenate([joined[:, :, :, 1:], right_rim], axis=3)
    lower_rim = shifted(joined[:, :, :1, :], "row", -1)
    joined = jnp.concatenate([joined[:, :, 1:, :], lower_rim], axis=2)
    return (
        joined[:, :out_ch],
        joined[:, out_ch:],
        cond_grad,
        g_patch,
        g_qkv.astype(F32),
        g_proj.astype(F32),
        g_up.astype(F32),
        g_down,
        g_ada,
        g_fada,
        g_out,
    )


def solution(mesh):
    rows = P("img", None)
    tile = P("img", None, "row", "col")
    whole = P("img", None, None)
    return jax.shard_map(
        local,
        mesh=mesh,
        in_specs=(tile, tile, whole, P("img")) + (rows,) * 8,
        out_specs=(tile, tile, whole) + (rows,) * 8,
        check_vma=False,
    )
```

```python
import math

import jax
import jax.numpy as jnp
from jax import lax
from jax.experimental import pallas as pl
from jax.experimental.pallas import tpu as pltpu
from jax.sharding import PartitionSpec as P

HEADS = 16
RC = ("row", "col")
BF = jnp.bfloat16
F32 = jnp.float32


def shifted(block, axis, distance):
    size = lax.axis_size(axis)
    return lax.ppermute(block, axis, [((i - distance) % size, i) for i in range(size)])


def layer_norm(value):
    center = value - jnp.mean(value, -1, keepdims=True)
    spread = jnp.mean(center * center, -1, keepdims=True)
    return center * lax.rsqrt(spread + 1e-06)


def modulate(value, shift, scale):
    return layer_norm(value) * (1.0 + scale[:, None, :]) + shift[:, None, :]


def gelu_tanh(value):
    return jax.nn.gelu(value, approximate=True)


def swish(value):
    return value * jax.nn.sigmoid(value)


def sincos(coord, count):
    freqs = 1.0 / 10000.0 ** (jnp.arange(count, dtype=F32) / count)
    angle = coord.astype(F32)[..., None] * freqs
    return jnp.concatenate([jnp.sin(angle), jnp.cos(angle)], axis=-1)


def dotd(left, right, ldim, rdim):
    return lax.dot_general(
        left, right, (((ldim,), (rdim,)), ((), ())), preferred_element_type=F32
    )


def send_down(value, k):
    size = lax.axis_size("img")
    return lax.ppermute(value, "img", [(j, (j - k) % size) for j in range(size)])


def send_up(value, k):
    size = lax.axis_size("img")
    return lax.ppermute(value, "img", [(j, (j + k) % size) for j in range(size)])


def split_own(value, axis):
    size = lax.axis_size("img")
    me = lax.axis_index("img")
    width = value.shape[axis] // size
    blocks = [lax.slice_in_dim(value, i * width, (i + 1) * width, axis=axis) for i in range(size)]
    if size == 2:
        return [
            jnp.where(me == 0, blocks[0], blocks[1]),
            jnp.where(me == 0, blocks[1], blocks[0]),
        ]
    return [
        lax.dynamic_slice_in_dim(value, (me + k) % size * width, width, axis=axis)
        for k in range(size)
    ]


def join_own(items, axis):
    size = lax.axis_size("img")
    me = lax.axis_index("img")
    if size == 2:
        return jnp.concatenate(
            [jnp.where(me == 0, items[0], items[1]), jnp.where(me == 0, items[1], items[0])],
            axis=axis,
        )
    width = items[0].shape[axis]
    twice = jnp.concatenate(list(items) + list(items), axis=axis)
    return lax.dynamic_slice_in_dim(twice, (size - me) % size * width, size * width, axis=axis)


def tied(value, *after):
    return lax.optimization_barrier((value, after))[0]


def swap_parts(parts):
    size = len(parts)
    return [parts[0]] + [send_down(parts[size - k], k) for k in range(1, size)]


def swap_full(value):
    return [value] + [send_down(value, k) for k in range(1, lax.axis_size("img"))]


def other_rows(weight):
    size = lax.axis_size("img")
    tiles = lax.axis_size("row") * lax.axis_size("col")
    at = lax.axis_index("row") * lax.axis_size("col") + lax.axis_index("col")
    rows, width = weight.shape
    each = -(-rows // (tiles * 8)) * 8
    start = jnp.minimum(at * each, rows - each)
    piece = lax.dynamic_slice(weight, (start, 0), (each, width))
    if rows % each:
        lag = jnp.clip(at * each - start, 0, each)
        piece = lax.dynamic_slice(jnp.concatenate([piece, piece], 0), (lag, 0), (each, width))
    pieces = [send_down(piece, k) for k in range(1, size)]
    if size == 2:
        return [lax.all_gather(pieces[0], RC, axis=0, tiled=True)], pieces
    full = lax.all_gather(jnp.stack(pieces), RC, axis=1, tiled=True)
    return [full[k] for k in range(size - 1)], pieces


def widened(part, rows, axis):
    extra = rows - part.shape[axis]
    if extra == 0:
        return part
    pads = [(0, 0), (0, 0)]
    pads[axis] = (0, extra)
    return jnp.pad(part, pads)


def quad_order(rows_n, cols_n):
    def quad(s):
        return s // cols_n * 2 // rows_n * 2 + s % cols_n * 2 // cols_n

    return sorted(range(rows_n * cols_n), key=quad)


def pick_tokens(pieces, par, half):
    lane = lax.broadcasted_iota(jnp.int32, pieces[0].shape, 1)
    tiles = []
    for j in range(0, len(pieces), 2):
        a = pieces[j].astype(F32)
        b = pieces[j + 1].astype(F32)
        if par == 0:
            tile = jnp.where(lane < half, a, pltpu.roll(b, half, 1))
        else:
            tile = jnp.where(lane < half, pltpu.roll(a, half, 1), b)
        tiles.append(tile.astype(BF))
    return jnp.concatenate(tiles, axis=1)


def put_tokens(first, second, spot, half):
    tile = spot // 2
    a = first[:, tile * 2 * half : (tile + 1) * 2 * half]
    b = second[:, tile * 2 * half : (tile + 1) * 2 * half]
    lane = lax.broadcasted_iota(jnp.int32, a.shape, 1)
    if spot % 2 == 0:
        return jnp.where(lane < half, a, pltpu.roll(b, half, 1))
    return jnp.where(lane < half, pltpu.roll(a, half, 1), b)


def attend_kernel(order, half, factor, kind_ref, x_ref, o_ref, lse_ref, qkv_s, o_s):
    step = pl.program_id(1)
    count = len(order) * half
    block = count // 4
    coef = factor * math.log2(math.e)
    for par in range(2):
        for c in range(3):
            qkv_s[c] = pick_tokens([x_ref[s, 0, c] for s in order], par, half)
        single = kind_ref[2 * step + par] == 0
        for b in range(4):
            cols = slice(b * block, (b + 1) * block)

            def work(keys, cols=cols, par=par):
                query = qkv_s[0, :, cols]
                score = dotd(qkv_s[1, :, keys], query, 0, 0)
                top = jnp.max(score, axis=0, keepdims=True)
                expd = jnp.exp2((score - top) * coef)
                total = jnp.sum(expd, axis=0, keepdims=True)
                out = dotd(qkv_s[2, :, keys], expd.astype(BF), 1, 0)
                o_s[par, :, cols] = out * (1.0 / total)
                lse_ref[0, par, :, cols] = top * coef + jnp.log2(total)

            @pl.when(single)
            def _():
                work(slice(0, count))

            @pl.when(jnp.logical_not(single))
            def _():
                work(cols)

    for i, s in enumerate(order):
        o_ref[s, 0] = put_tokens(o_s[0], o_s[1], i, half).astype(BF)


def attend_back_kernel(
    order, half, factor, kind_ref, x_ref, d_ref, o_ref, lse_ref, g_ref, qkv_s, d_s, e_s, g_s
):
    step = pl.program_id(1)
    count = len(order) * half
    block = count // 4
    coef = factor * math.log2(math.e)
    for par in range(2):
        for c in range(3):
            qkv_s[c] = pick_tokens([x_ref[s, 0, c] for s in order], par, half)
        dout_all = pick_tokens([d_ref[s, 0] for s in order], par, half)
        out_all = pick_tokens([o_ref[s, 0] for s in order], par, half)
        d_s[...] = dout_all
        e_s[...] = jnp.sum(dout_all.astype(F32) * out_all.astype(F32), axis=0, keepdims=True)
        single = kind_ref[2 * step + par] == 0
        for b in range(4):
            cols = slice(b * block, (b + 1) * block)

            def work(keys, fresh, cols=cols, par=par):
                query = qkv_s[0, :, cols]
                dout = d_s[:, cols]
                score = dotd(qkv_s[1, :, keys], query, 0, 0)
                prob = jnp.exp2(score * coef - lse_ref[0, par, :, cols])
                dprob = dotd(qkv_s[2, :, keys], dout, 0, 0)
                dscore = (prob * (dprob - e_s[:, cols])).astype(BF)
                g_s[par, 0, :, cols] = dotd(qkv_s[1, :, keys], dscore, 1, 0) * factor
                dkey = dotd(query, dscore, 1, 1) * factor
                dvalue = dotd(dout, prob.astype(BF), 1, 1)
                if fresh:
                    g_s[par, 1, :, keys] = dkey
                    g_s[par, 2, :, keys] = dvalue
                else:
                    g_s[par, 1, :, keys] += dkey
                    g_s[par, 2, :, keys] += dvalue

            @pl.when(single)
            def _():
                work(slice(0, count), b == 0)

            @pl.when(jnp.logical_not(single))
            def _():
                work(cols, True)

    for c in range(3):
        for i, s in enumerate(order):
            g_ref[s, 0, c] = put_tokens(g_s[0, c], g_s[1, c], i, half).astype(BF)


def attend(kinds, x, order, half, factor):
    tiles, per, _, depth, tokens = x.shape
    count = tiles * half
    pairs = tokens // (2 * half)
    return pl.pallas_call(
        lambda *refs: attend_kernel(order, half, factor, *refs),
        grid_spec=pltpu.PrefetchScalarGridSpec(
            num_scalar_prefetch=1,
            grid=(per, pairs),
            in_specs=[
                pl.BlockSpec((tiles, 1, 3, depth, 2 * half), lambda h, p, kd: (0, h, 0, 0, p))
            ],
            out_specs=[
                pl.BlockSpec((tiles, 1, depth, 2 * half), lambda h, p, kd: (0, h, 0, p)),
                pl.BlockSpec((1, 2, 1, count), lambda h, p, kd: (h, p, 0, 0)),
            ],
            scratch_shapes=[
                pltpu.VMEM((3, depth, count), BF),
                pltpu.VMEM((2, depth, count), F32),
            ],
        ),
        out_shape=[
            jax.ShapeDtypeStruct((tiles, per, depth, tokens), BF),
            jax.ShapeDtypeStruct((per, 2 * pairs, 1, count), F32),
        ],
        name="attend",
        cost_estimate=pl.CostEstimate(
            flops=10**10, bytes_accessed=4 * 10**7, transcendentals=per * tokens * count
        ),
    )(kinds, x)


def attend_back(kinds, x, d, o, lse, order, half, factor):
    tiles, per, _, depth, tokens = x.shape
    count = tiles * half
    pairs = tokens // (2 * half)
    return pl.pallas_call(
        lambda *refs: attend_back_kernel(order, half, factor, *refs),
        grid_spec=pltpu.PrefetchScalarGridSpec(
            num_scalar_prefetch=1,
            grid=(per, pairs),
            in_specs=[
                pl.BlockSpec((tiles, 1, 3, depth, 2 * half), lambda h, p, kd: (0, h, 0, 0, p)),
                pl.BlockSpec((tiles, 1, depth, 2 * half), lambda h, p, kd: (0, h, 0, p)),
                pl.BlockSpec((tiles, 1, depth, 2 * half), lambda h, p, kd: (0, h, 0, p)),
                pl.BlockSpec((1, 2, 1, count), lambda h, p, kd: (h, p, 0, 0)),
            ],
            out_specs=pl.BlockSpec(
                (tiles, 1, 3, depth, 2 * half), lambda h, p, kd: (0, h, 0, 0, p)
            ),
            scratch_shapes=[
                pltpu.VMEM((3, depth, count), BF),
                pltpu.VMEM((depth, count), BF),
                pltpu.VMEM((1, count), F32),
                pltpu.VMEM((2, 3, depth, count), F32),
            ],
        ),
        out_shape=jax.ShapeDtypeStruct(x.shape, BF),
        name="attend_back",
        cost_estimate=pl.CostEstimate(
            flops=10**10, bytes_accessed=4 * 10**7, transcendentals=per * tokens * count
        ),
    )(kinds, x, d, o, lse)


def swapped(value, axis, bit):
    return lax.ppermute(value, axis, [(j, j ^ bit) for j in range(lax.axis_size(axis))])


def added(a, b):
    return (a.astype(F32) + b.astype(F32)).astype(BF)


def halved(value, axis, bit):
    upper = lax.axis_index(axis) // bit % 2
    rows = value.shape[0] // 2
    keep = lax.dynamic_slice_in_dim(value, upper * rows, rows, 0)
    give = lax.dynamic_slice_in_dim(value, (1 - upper) * rows, rows, 0)
    return added(keep, swapped(give, axis, bit))


def doubled(value, axis, bit):
    upper = lax.axis_index(axis) // bit % 2
    got = swapped(value, axis, bit)
    return jnp.where(
        upper == 0, jnp.concatenate([value, got], 0), jnp.concatenate([got, value], 0)
    )


def bits_of(axis):
    return [(axis, 1 << i) for i in range(lax.axis_size(axis).bit_length() - 1)]


def tile_halved(value):
    bits = bits_of("row") + bits_of("col")
    for axis, bit in bits[:-1]:
        value = halved(value, axis, bit)
    axis, bit = bits[-1]
    return added(value, swapped(value, axis, bit))


def tile_doubled(value):
    bits = bits_of("row") + bits_of("col")
    for axis, bit in bits[-2::-1]:
        value = doubled(value, axis, bit)
    return value


def exchange(x):
    return lax.all_to_all(x, RC, split_axis=0, concat_axis=0, tiled=True)


def blank(shape, dtype):
    return pl.pallas_call(
        lambda ref: None,
        out_specs=pl.BlockSpec(memory_space=pl.ANY),
        out_shape=jax.ShapeDtypeStruct(shape, dtype),
        name="blank",
    )()


def summed_apart(small, items, finish):
    once = 1 + jnp.minimum(lax.axis_index("row"), 0)
    tiles, each, width = small.shape
    imgs = lax.axis_size("img")

    def body(_, state):
        parts = jnp.sum(exchange(state[0]).astype(F32), axis=0).astype(BF)
        parts = jnp.stack(swap_full(parts))
        parts = exchange(jnp.broadcast_to(parts[None], (tiles,) + parts.shape))
        parts = parts.transpose(1, 0, 2, 3)
        done = finish(parts.reshape(imgs, tiles * each, width))
        sums = [tile_halved(value) for value in state[1]]
        late = len(sums) // 2
        sums[late:], done = lax.optimization_barrier((sums[late:], done))
        return parts[0], [tile_doubled(value) for value in sums], done

    empty = jax.eval_shape(finish, jax.ShapeDtypeStruct((imgs, tiles * each, width), BF))
    empty = jax.tree.map(lambda item: blank(item.shape, item.dtype), empty)
    return lax.fori_loop(0, once, body, (small, items, empty))[1:]


def outer_kernel(left_ref, right_ref, out_ref):
    out_ref[...] = dotd(left_ref[...], right_ref[...], 0, 0)


def outer(left, right, block):
    depth, rows = left.shape
    cols = right.shape[1]
    return pl.pallas_call(
        outer_kernel,
        grid=(cols // block,),
        in_specs=[
            pl.BlockSpec((depth, rows), lambda j: (0, 0)),
            pl.BlockSpec((depth, block), lambda j: (0, j)),
        ],
        out_specs=pl.BlockSpec((rows, block), lambda j: (0, j)),
        out_shape=jax.ShapeDtypeStruct((rows, cols), F32),
        name="outer",
    )(left, right)


def local(
    latent,
    cotangent,
    cond,
    canvas_kind,
    w_patch,
    w_qkv,
    w_proj,
    w_up,
    w_down,
    w_ada,
    w_final_ada,
    w_out,
):
    local_n, chans, tile_r, tile_c = latent.shape
    out_ch = cotangent.shape[1]
    slots = cond.shape[1]
    width = cond.shape[2]
    inner = w_up.shape[1]
    imgs = lax.axis_size("img")
    rows_n = lax.axis_size("row")
    cols_n = lax.axis_size("col")
    row_at = lax.axis_index("row")
    col_at = lax.axis_index("col")
    tiles = rows_n * cols_n
    patch_r = tile_r // 2
    patch_c = tile_c // 2
    tile_tok = patch_r * patch_c
    half = patch_r * rows_n // 2
    half_c = patch_c * cols_n // 2
    head_dim = width // HEADS
    per = HEADS // tiles
    factor = head_dim ** (-0.5)
    rows = local_n * tile_tok
    order = quad_order(rows_n, cols_n)

    o_qkv, sent = other_rows(w_qkv)
    o_up, sent = other_rows(tied(w_up, sent))
    lower = w_down.shape[0] // 3
    w_straight = tied(w_down[:lower], sent)
    o_low = [send_down(w_straight, k) for k in range(1, imgs)]
    w_straight = tied(w_down[lower : 2 * lower], o_low)
    o_mid = [send_down(w_straight, k) for k in range(1, imgs)]
    wp = join_own([w_patch] + [send_down(w_patch, k) for k in range(1, imgs)], 0)
    wout = join_own([w_out] + [send_down(w_out, k) for k in range(1, imgs)], 0)

    stacked = jnp.concatenate([latent, cotangent], axis=1)
    upper = shifted(stacked[:, :, -1:, :], "row", 1)
    framed = jnp.concatenate([upper, stacked[:, :, :-1, :]], axis=2)
    beside = shifted(framed[:, :, :, -1:], "col", 1)
    framed = jnp.concatenate([beside, framed[:, :, :, :-1]], axis=3)

    def to_tokens(tile):
        depth = tile.shape[1]
        shaped = tile.reshape(local_n, depth, patch_r, 2, patch_c, 2).transpose(0, 2, 4, 1, 3, 5)
        return shaped.reshape(rows, depth * 4)

    def to_tile(tokens):
        depth = tokens.shape[1] // 4
        shaped = tokens.reshape(local_n, patch_r, patch_c, depth, 2, 2).transpose(0, 3, 1, 4, 2, 5)
        return shaped.reshape(local_n, depth, tile_r, tile_c)

    pieces = to_tokens(framed[:, :chans])
    dout = to_tokens(framed[:, chans:])

    quad = row_at * 2 // rows_n * 2 + col_at * 2 // cols_n
    slot = canvas_kind * quad
    picker = (slot[:, None] == jnp.arange(slots, dtype=jnp.int32)[None, :]).astype(F32)
    silu = swish(cond)
    silu_low = silu.astype(BF)
    chosen = jnp.sum(picker[:, :, None] * silu_low.astype(F32), axis=1).astype(BF)
    packed = jnp.concatenate([chosen, silu_low.reshape(local_n * slots, width)], axis=0)
    packed = swap_parts(split_own(packed, 1))
    silu_all = jnp.concatenate([item[local_n:] for item in packed], axis=0)
    chosen_all = jnp.concatenate([item[:local_n] for item in packed], axis=0)
    part = jnp.concatenate(
        [dotd(chosen_all, w_ada, 1, 0), dotd(chosen_all, w_final_ada, 1, 0)], axis=1
    )
    part = [part[k * local_n : (k + 1) * local_n] for k in range(imgs)]
    mods = part[0]
    for k in range(1, imgs):
        mods = mods + send_up(part[k], k)
    shift1, scale1, gate1, shift2, scale2, gate2, shiftf, scalef = jnp.split(mods, 8, axis=-1)

    prow = row_at * patch_r + jnp.arange(patch_r, dtype=jnp.int32)
    pcol = col_at * patch_c + jnp.arange(patch_c, dtype=jnp.int32)
    lrow = prow[None, :] - canvas_kind[:, None] * (prow[None, :] // half) * half
    lcol = pcol[None, :] - canvas_kind[:, None] * (pcol[None, :] // half_c) * half_c
    table_r = sincos(lrow, width // 4)
    table_c = sincos(lcol, width // 4)
    full = (local_n, patch_r, patch_c, width // 2)
    positions = jnp.concatenate(
        [
            jnp.broadcast_to(table_c[:, None, :, :], full),
            jnp.broadcast_to(table_r[:, :, None, :], full),
        ],
        axis=-1,
    ).reshape(local_n, tile_tok, width)

    def tokens3(value):
        return value.reshape(local_n, tile_tok, -1)

    x0 = tokens3(dotd(pieces, wp, 1, 0)) + positions
    a1 = modulate(x0, shift1, scale1).astype(BF).reshape(rows, width)
    o_proj, _ = other_rows(tied(w_proj, a1))
    o_high, _ = other_rows(tied(w_down[2 * lower :], a1))
    a1_parts = split_own(a1, 1)
    a1_all = jnp.concatenate(swap_parts(a1_parts), 0)

    def product(parts, own, others):
        total = dotd(parts[0], own, 1, 0)
        for part, other in zip(parts[1:], others):
            total = total + dotd(widened(part, other.shape[0], 1), other, 1, 0)
        return total

    def back_product(value, own, others):
        items = [dotd(value, own, 1, 1)]
        for other in others:
            items.append(dotd(value, other, 1, 1)[:, : own.shape[0]])
        return items

    qkv = dotd(w_qkv, a1_parts[0], 0, 1)
    for part, other in zip(a1_parts[1:], o_qkv):
        qkv = qkv + dotd(other, widened(part, other.shape[0], 1), 0, 1)
    qkv = qkv.astype(BF).reshape(3, tiles, per, head_dim, rows).transpose(1, 2, 0, 3, 4)
    qkv = exchange(qkv)
    qkv, o_low = lax.optimization_barrier((qkv, o_low))
    att, lse = attend(canvas_kind, qkv, order, tile_tok, factor)
    att_head = att
    att = exchange(att).reshape(width, rows)
    att, a1_all, o_mid = lax.optimization_barrier((att, a1_all, o_mid))
    att_parts = split_own(att, 0)
    att_all = jnp.concatenate(swap_parts(att_parts), 1)
    proj = dotd(att_parts[0], w_proj, 0, 0)
    for part, other in zip(att_parts[1:], o_proj):
        proj = proj + dotd(widened(part, other.shape[0], 0), other, 0, 0)
    proj = tokens3(proj)
    x1 = x0 + gate1[:, None, :] * proj
    a2 = modulate(x1, shift2, scale2).astype(BF).reshape(rows, width)
    a2_parts = split_own(a2, 1)
    a2_all = jnp.concatenate(swap_parts(a2_parts), 0)
    pre = product(a2_parts, w_up, o_up)
    hid = gelu_tanh(pre).astype(BF)
    hid, att_all, a2_all = lax.optimization_barrier((hid, att_all, a2_all))
    hid_parts = split_own(hid, 1)
    hid_all = swap_parts(hid_parts)
    down = dotd(hid_parts[0], w_down, 1, 0)
    for part, low, mid, high in zip(hid_parts[1:], o_low, o_mid, o_high):
        straight = jnp.concatenate([low, mid], axis=0)
        down = down + dotd(part[:, : 2 * lower], straight, 1, 0)
        down = down + dotd(widened(part[:, 2 * lower :], high.shape[0], 1), high, 1, 0)
    down = tokens3(down)
    x2 = x1 + gate2[:, None, :] * down
    af = modulate(x2, shiftf, scalef).astype(BF).reshape(rows, width)
    outp = dotd(af, wout, 1, 0)

    g_out = dotd(dout, af, 0, 0)
    daf = tokens3(dotd(dout, wout, 1, 1))
    _, pull = jax.vjp(modulate, x2, shiftf, scalef)
    dx2, dshiftf, dscalef = pull(daf)
    dgate2 = jnp.sum(dx2 * down, axis=1)
    ddown = (gate2[:, None, :] * dx2).astype(BF).reshape(rows, width)
    ddown_all = swap_full(ddown)
    dhid = [dotd(ddown, w_down, 1, 1)]
    for low, mid, high in zip(o_low, o_mid, o_high):
        straight = jnp.concatenate([low, mid], axis=0)
        last = w_down.shape[0] - 2 * lower
        items = [dotd(ddown, straight, 1, 1), dotd(ddown, high, 1, 1)[:, :last]]
        dhid.append(jnp.concatenate(items, axis=1))
    dhid = join_own(dhid, 1)
    _, pull = jax.vjp(gelu_tanh, pre)
    dpre = pull(dhid)[0].astype(BF)
    dpre_all = swap_full(dpre)
    da2 = tokens3(join_own(back_product(dpre, w_up, o_up), 1))
    da2, hid_all, ddown_all = lax.optimization_barrier((da2, hid_all, ddown_all))
    g_down = dotd(jnp.concatenate(hid_all, 0), jnp.concatenate(ddown_all, 0), 0, 0).astype(BF)
    da2, g_down = lax.optimization_barrier((da2, g_down))
    g_down = lax.psum_scatter(g_down, RC, scatter_dimension=0, tiled=True)
    _, pull = jax.vjp(modulate, x1, shift2, scale2)
    dx1_norm, dshift2, dscale2 = pull(da2)
    dx1 = dx2 + dx1_norm
    dgate1 = jnp.sum(dx1 * proj, axis=1)
    dproj = (gate1[:, None, :] * dx1).astype(BF).reshape(rows, width)
    datt = [dotd(w_proj, dproj, 1, 1)]
    for other in o_proj:
        datt.append(dotd(other, dproj, 1, 1)[: w_proj.shape[0]])
    datt = join_own(datt, 0).astype(BF)
    datt = exchange(datt.reshape(tiles, per, head_dim, rows))
    dproj_all = jnp.concatenate(swap_full(dproj), 0)
    dqkv = attend_back(canvas_kind, qkv, datt, att_head, lse, order, tile_tok, factor)
    dqkv, dpre_all = lax.optimization_barrier((dqkv, dpre_all))
    dqkv = exchange(dqkv)
    g_up = dotd(a2_all, jnp.concatenate(dpre_all, 0), 0, 0).astype(BF)
    g_proj = dotd(att_all, dproj_all, 1, 0).astype(BF)
    dqkv, g_up, g_down, g_proj, outp, g_out = lax.optimization_barrier(
        (dqkv, g_up, g_down, g_proj, outp, g_out)
    )
    g_down = lax.all_gather(g_down, RC, axis=0, tiled=True)
    dqkv = dqkv.transpose(2, 0, 1, 3, 4).reshape(3 * width, rows)
    dqkv_all = jnp.concatenate(swap_full(dqkv), 1)
    g_up, g_down = lax.optimization_barrier((g_up, g_down))
    g_up = lax.psum(g_up, RC)
    da1 = [dotd(dqkv, w_qkv, 0, 1)]
    for other in o_qkv:
        da1.append(dotd(dqkv, other, 0, 1)[:, : w_qkv.shape[0]])
    da1 = tokens3(join_own(da1, 1))
    g_att = [
        dotd(a1_all, dqkv_all[c * width : (c + 1) * width], 0, 1).astype(BF) for c in range(3)
    ]
    _, pull = jax.vjp(modulate, x0, shift1, scale1)
    dx0_norm, dshift1, dscale1 = pull(da1)
    dtok = (dx1 + dx0_norm).astype(BF).reshape(rows, width)
    g_patch = dotd(pieces, dtok, 0, 0)
    dpatch = dotd(dtok, wp, 1, 1)

    dmods = jnp.concatenate(
        [dshift1, dscale1, dgate1, dshift2, dscale2, dgate2, dshiftf, dscalef], axis=-1
    )
    dmods = (picker[:, :, None] * dmods[:, None, :]).reshape(local_n * slots * 8, width)
    small = jnp.concatenate([g_patch, g_out, dmods], axis=0)
    n_patch = g_patch.shape[0]
    n_out = g_out.shape[0]
    count = small.shape[0]
    each = -(-count // tiles)
    small = jnp.pad(small, ((0, each * tiles - count), (0, 0))).astype(BF)
    step = local_n * slots

    def split_small(value):
        return value[:, n_patch + n_out : count].reshape(imgs * step, 8 * width)

    def finish(value):
        sums = jnp.sum(value[:, : n_patch + n_out].astype(F32), axis=0)
        dmods = split_small(value)
        dsilu = dotd(dmods[:, : 6 * width], w_ada, 1, 1)
        dsilu = dsilu + dotd(dmods[:, 6 * width :], w_final_ada, 1, 1)
        dsilu = [dsilu[k * step : (k + 1) * step] for k in range(imgs)]
        dsilu = [dsilu[0]] + [send_up(dsilu[imgs - k], imgs - k) for k in range(1, imgs)]
        return (
            sums,
            join_own(dsilu, 1),
            outer(silu_all, dmods[:, : 6 * width], width),
            outer(silu_all, dmods[:, 6 * width :], width),
            g_down.astype(F32),
        )

    g_att, done = summed_apart(small.reshape(tiles, each, width), g_att + [g_proj], finish)
    sums, dsilu, g_ada, g_fada, g_down = done
    g_qkv = jnp.concatenate(g_att[:3], axis=1)
    g_proj = g_att[3]
    g_patch = split_own(sums[:n_patch], 0)[0]
    g_out = split_own(sums[n_patch:], 1)[0].T
    dsilu = dsilu.reshape(local_n, slots, width)
    _, pull = jax.vjp(swish, cond)
    cond_grad = pull(dsilu)[0]

    joined = jnp.concatenate([to_tile(outp), to_tile(dpatch)], axis=1)
    right_rim = shifted(joined[:, :, :, :1], "col", -1)
    joined = jnp.concatenate([joined[:, :, :, 1:], right_rim], axis=3)
    lower_rim = shifted(joined[:, :, :1, :], "row", -1)
    joined = jnp.concatenate([joined[:, :, 1:, :], lower_rim], axis=2)
    return (
        joined[:, :out_ch],
        joined[:, out_ch:],
        cond_grad,
        g_patch,
        g_qkv.astype(F32),
        g_proj.astype(F32),
        g_up.astype(F32),
        g_down,
        g_ada,
        g_fada,
        g_out,
    )


def solution(mesh):
    rows = P("img", None)
    tile = P("img", None, "row", "col")
    whole = P("img", None, None)
    return jax.shard_map(
        local,
        mesh=mesh,
        in_specs=(tile, tile, whole, P("img")) + (rows,) * 8,
        out_specs=(tile, tile, whole) + (rows,) * 8,
        check_vma=False,
    )
```
